128 devices in a mesh: recv: 16 (over y, z), send: 8 (over x, core).
Axes of the slice: x: 4, y: 4, z: 4, core: 2. Of those that a mesh axis runs over, the one named last changes fastest.
Arguments:
- nodes: bfloat16 [8192, 256], P('recv'), may hold values from -24 to 24
- frames: int32 [8192], replicated, may hold values from 0 to 59, never falling along the last dimension, each value on 1 to 512 neighbouring positions
- pairs: int32 [2, 512], P(None, ('recv', 'send')), may hold values from 0 to 63, as said below
- masks: int32 [512, 128], P(('recv', 'send')), may hold values from 0 to 1, as said below
- d_out: bfloat16 [8192, 256], P('recv'), may hold values from -6 to 6
- w_query: bfloat16 [256, 256], replicated, may hold values from -0.375 to 0.375
- w_key: bfloat16 [256, 256], replicated, may hold values from -0.375 to 0.375
- w_value: bfloat16 [256, 256], replicated, may hold values from -0.375 to 0.375
- w_left: bfloat16 [256, 128], replicated, may hold values from -0.375 to 0.375
- w_right: bfloat16 [256, 128], replicated, may hold values from -0.375 to 0.375
- frame_edge: bfloat16 [128], replicated, may hold values from -4 to 4
- w_bias: bfloat16 [8, 128], replicated, may hold values from -0.5 to 0.5
- w_edge_value: bfloat16 [128, 256], replicated, may hold values from -0.5 to 0.5
- w_out: bfloat16 [256, 256], replicated, may hold values from -0.375 to 0.375
Outputs:
- mixed: bfloat16 [8192, 256], P('recv')
- grad_nodes: float32 [8192, 256], P('recv')
- grad_bias: float32 [8, 128], replicated
- grad_edge_value: float32 [128, 256], replicated
The draws below stay inside these ranges and needn't reach their ends.
Inputs may be any that keep to these rules, and one draw needn't show every extreme that they name: `pairs`: row 0 holds a slot's receiver block, row 1 its sender block; block b belongs to recv index b // 4. The slots of the device at recv index r have receiver blocks r * 4 to r * 4 + 3. The sender blocks of one receiver block are distinct over all its slots and include the block itself, in a slot at send index 0. On each device, the slots whose sender block belongs to another recv index name blocks of distinct recv indices. `masks`: A slot that pairs a block with itself is all ones; other slots may be all zeros. `frames`: frame ids never fall along the residues; every frame holds a residue.
All inputs are finite; a program needn't handle non-finite values.
Results may differ from the reference program's by a relative error of at most 0.039.
Values may be sent and summed in bfloat16 or wider, within the bound.
No kernel may reach another device: no remote copies, remote signals or barrier semaphores. Data moves between devices by JAX's collectives and lax.ppermute only.
A program may use at most 128 MiB of HBM per device.

```python
import math
import jax
import jax.numpy as jnp
import numpy as np
from jax import lax

D = 256
E = 128
HEADS = 8
HEAD_DIM = 32
BLK = 128
FRAMES = 60
NB_DEV = 4
PAIRS_DEV = 4
NBLK = 64
NODES = 8192
SLOTS = 512
ATT_WIDTH = 256


def slot_layout():
    n_recv = NBLK // NB_DEV
    n_send = SLOTS // (PAIRS_DEV * n_recv)
    slot_index = jnp.arange(SLOTS, dtype=jnp.int32)
    device = slot_index // PAIRS_DEV
    within = slot_index % PAIRS_DEV
    recv_index = device // n_send
    send_index = device % n_send
    recv_block = recv_index * NB_DEV + within % NB_DEV
    slot_rank = send_index * (PAIRS_DEV // NB_DEV) + within // NB_DEV
    return (recv_block, slot_rank, recv_index, send_index, within)


def draw_pairs(key, part):
    n_recv = NBLK // NB_DEV
    recv_block, slot_rank, recv_index, send_index, within = slot_layout()
    spread = send_index * PAIRS_DEV + within - NB_DEV
    is_self = spread < 0
    offset_base = jnp.maximum(spread, 0)
    offset_rank = offset_base % (n_recv - 1)
    cycle = offset_base // (n_recv - 1)
    coin_bits = jax.random.randint(jax.random.fold_in(key, 11), (n_recv, n_recv - 1), 0, 1 << 20)
    column = jnp.arange(n_recv - 1, dtype=jnp.int32)
    scores = coin_bits * (n_recv - 1) + column[None, :]
    order = jnp.argsort(scores, axis=1, stable=True).astype(jnp.int32)
    offset = order[recv_index, offset_rank] + 1
    turn = jax.random.randint(jax.random.fold_in(key, 12), (NBLK,), 0, NB_DEV)
    owner = (recv_index + offset) % n_recv
    member = (cycle + turn[recv_block]) % NB_DEV
    send_block = jnp.where(is_self, recv_block, owner * NB_DEV + member)
    return jnp.stack([recv_block, send_block]).astype(jnp.int32)


def draw_masks(key, part):
    recv_block, slot_rank, recv_index, send_index, within = slot_layout()
    empty = jax.random.randint(jax.random.fold_in(key, 21), (SLOTS,), 0, 5) < 2
    live = jax.random.randint(jax.random.fold_in(key, 22), (SLOTS, BLK), 0, 4) < 3
    live = jnp.where(empty[:, None], False, live)
    live = jnp.where((slot_rank == 0)[:, None], True, live)
    return live.astype(jnp.int32)


def draw_nodes(key, part):
    return jnp.clip(jax.random.normal(jax.random.fold_in(key, 33), (NODES, D), jnp.float32), -6.0, 6.0).astype(jnp.bfloat16)


def query_key_base(key):
    first = jnp.clip(jax.random.normal(jax.random.fold_in(key, 41), (D, ATT_WIDTH), jnp.float32), -6.0, 6.0)
    second = jnp.clip(jax.random.normal(jax.random.fold_in(key, 42), (D, ATT_WIDTH), jnp.float32), -6.0, 6.0)
    return (first, second)


def draw_w_query(key, part):
    first, second = query_key_base(key)
    return (first * D ** (-0.5)).astype(jnp.bfloat16)


def draw_w_key(key, part):
    first, second = query_key_base(key)
    joined = second
    return (joined * D ** (-0.5)).astype(jnp.bfloat16)


def level_of(own_key, dims, cuts, least, top_value):
    def one(position, blocks):
        draws = jax.random.uniform(jax.random.fold_in(jax.random.fold_in(own_key, 6), position), (blocks,), jnp.float32, least / len(cuts), top_value / len(cuts))
        return jnp.repeat(jnp.exp(draws), dims[position] // blocks).reshape((-1,) + (1,) * (len(dims) - position - 1))

    loudness = one(*cuts[0])
    for cut in cuts[1:]:
        loudness = loudness * one(*cut)
    return loudness


def split_up(amount, total, limit, slope):
    portions = [(1 << 20) // math.isqrt(grade ** slope) + 1 for grade in range(2, amount + 1)]
    spare, holding = total - limit - (amount - 1), [1] * (amount - 1)
    while spare > 0:
        free = [i for i in range(amount - 1) if holding[i] < limit]
        whole, left = sum([portions[i] for i in free]), spare
        for i in free:
            extra = min(limit - holding[i], max(1, left * portions[i] // whole), spare)
            holding[i] = holding[i] + extra
            spare = spare - extra
    return np.array([limit] + holding)


def uneven_parts(stream_key, amount, total, bound, lean):
    if amount == 2:
        one = jax.random.randint(stream_key, (), max(1, total - bound), min(bound, total - 1) + 1)
        return jnp.stack([one, total - one])
    lengths = jnp.asarray(split_up(amount, total, bound, lean), jnp.int32)
    couples = (amount - 1) // 2
    giver, taker = lengths[1:1 + 2 * couples:2], lengths[2:2 + 2 * couples:2]
    slack = jnp.minimum(giver - 1, bound - taker)
    shifted = jax.random.randint(jax.random.fold_in(stream_key, 1), (couples,), 0, 1 << 20) % (slack + 1)
    lengths = lengths.at[1:1 + 2 * couples:2].set(giver - shifted).at[2:2 + 2 * couples:2].set(taker + shifted)
    return lengths[jax.random.permutation(jax.random.fold_in(stream_key, 2), amount)]


def bell_draw(rng, dims, width, most, pieces=(), held_as=jnp.bfloat16):
    level = level_of(rng, dims, pieces, -0.22, 0.18) if pieces else 1.0
    result = jax.random.normal(rng, dims, jnp.float32) * width * level
    return jnp.minimum(jnp.maximum(result, -most), most).astype(held_as)


def setup_inputs(seed: int = 0) -> dict:
    streams_of = jax.random.split(jax.random.key(seed), 15)
    return {
        "nodes": draw_nodes(jax.random.fold_in(streams_of[14], 71), 0),
        "frames": jnp.searchsorted(jnp.cumsum(uneven_parts(streams_of[1], FRAMES, NODES, NODES // 16, 0)), jnp.arange(NODES), side="right").astype(jnp.int32),
        "pairs": draw_pairs(jax.random.fold_in(streams_of[14], 71), 0),
        "masks": draw_masks(jax.random.fold_in(streams_of[14], 71), 0),
        "d_out": bell_draw(streams_of[4], (NODES, D), 1.0, 6.0, ((0, 16),)),
        "w_query": draw_w_query(jax.random.fold_in(streams_of[14], 71), 0),
        "w_key": draw_w_key(jax.random.fold_in(streams_of[14], 71), 0),
        "w_value": bell_draw(streams_of[7], (D, ATT_WIDTH), D ** -0.5, 0.375),
        "w_left": bell_draw(streams_of[8], (D, E), D ** -0.5, 0.375),
        "w_right": bell_draw(streams_of[9], (D, E), D ** -0.5, 0.375),
        "frame_edge": bell_draw(streams_of[10], (E,), 1.0, 4.0),
        "w_bias": bell_draw(streams_of[11], (HEADS, E), E ** -0.5, 0.5),
        "w_edge_value": bell_draw(streams_of[12], (E, ATT_WIDTH), E ** -0.5, 0.5),
        "w_out": bell_draw(streams_of[13], (ATT_WIDTH, D), ATT_WIDTH ** -0.5, 0.375),
    }


NEG_LARGE = -1.0e30


def highest(grad_rows, weight):
    return jnp.dot(grad_rows, weight.astype(jnp.float32).T, precision=lax.Precision.HIGHEST)


def add_rows(array, start, update):
    current = lax.dynamic_slice_in_dim(array, start, update.shape[0], 0)
    return lax.dynamic_update_slice_in_dim(array, current + update, start, 0)


def reference(nodes, frames, pairs, masks, d_out, w_query, w_key, w_value, w_left, w_right, frame_edge, w_bias, w_edge_value, w_out):
    def project(weight):
        return jnp.dot(nodes, weight, preferred_element_type=jnp.float32).astype(jnp.bfloat16)

    query = project(w_query)
    keys_all = project(w_key)
    values_all = project(w_value)
    left_all = project(w_left)
    right_all = project(w_right)
    scale = HEAD_DIM ** -0.5
    edge_gain = frame_edge.astype(jnp.float32)
    bias_weight = w_bias.astype(jnp.float32)

    def rows_of(array, start):
        return lax.dynamic_slice_in_dim(array, start, BLK, 0)

    def fetch(slot_at):
        recv_block = pairs[0, slot_at].astype(jnp.int32)
        send_block = pairs[1, slot_at].astype(jnp.int32)
        recv_start = (recv_block * BLK).astype(jnp.int32)
        send_start = (send_block * BLK).astype(jnp.int32)
        query_blk = rows_of(query, recv_start).astype(jnp.float32).reshape(BLK, HEADS, HEAD_DIM)
        keys_blk = rows_of(keys_all, send_start).astype(jnp.float32).reshape(BLK, HEADS, HEAD_DIM)
        values_blk = rows_of(values_all, send_start).astype(jnp.float32).reshape(BLK, HEADS, HEAD_DIM)
        same_frame = (rows_of(frames, recv_start)[:, None] == rows_of(frames, send_start)[None, :]).astype(jnp.float32)
        pre_act = (rows_of(left_all, recv_start).astype(jnp.float32)[:, None, :]
                   + rows_of(right_all, send_start).astype(jnp.float32)[None, :, :]
                   + same_frame[:, :, None] * edge_gain[None, None, :])
        edge_feat = jax.nn.silu(pre_act).astype(jnp.bfloat16)
        valid = masks[slot_at] > 0
        logits = jnp.einsum("ihd,jhd->hij", query_blk, keys_blk) * scale
        logits = logits + jnp.einsum("ije,he->hij", edge_feat.astype(jnp.float32), bias_weight)
        logits = jnp.where(valid[None, None, :], logits, NEG_LARGE)
        return recv_block, recv_start, send_start, query_blk, keys_blk, values_blk, pre_act, edge_feat, valid, logits

    def stats_step(carry, slot_at):
        row_top, row_total = carry
        recv_block, recv_start, send_start, query_blk, keys_blk, values_blk, pre_act, edge_feat, valid, logits = fetch(slot_at)
        slot_top = jnp.max(logits, axis=2)
        slot_total = jnp.sum(jnp.where(valid[None, None, :], jnp.exp(logits - slot_top[:, :, None]), 0.0), axis=2)
        old_top = row_top[recv_block]
        old_total = row_total[recv_block]
        new_top = jnp.maximum(old_top, slot_top)
        new_total = old_total * jnp.exp(old_top - new_top) + slot_total * jnp.exp(slot_top - new_top)
        return (row_top.at[recv_block].set(new_top), row_total.at[recv_block].set(new_total)), None

    slot_ids = jnp.arange(SLOTS, dtype=jnp.int32)
    start_stats = (jnp.full((NBLK, HEADS, BLK), NEG_LARGE, jnp.float32), jnp.zeros((NBLK, HEADS, BLK), jnp.float32))
    (row_top, row_total), _ = lax.scan(stats_step, start_stats, slot_ids)

    def probs_of(logits, valid, recv_block):
        return jnp.where(valid[None, None, :], jnp.exp(logits - row_top[recv_block][:, :, None]) / row_total[recv_block][:, :, None], 0.0)

    def sum_step(carry, slot_at):
        out_acc, ctx_acc = carry
        recv_block, recv_start, send_start, query_blk, keys_blk, values_blk, pre_act, edge_feat, valid, logits = fetch(slot_at)
        weights = probs_of(logits, valid, recv_block).astype(jnp.bfloat16).astype(jnp.float32)
        part_out = jnp.einsum("hij,jhd->ihd", weights, values_blk).reshape(BLK, ATT_WIDTH)
        part_ctx = jnp.einsum("hij,ije->ihe", weights, edge_feat.astype(jnp.float32)).reshape(BLK, HEADS * E)
        return (add_rows(out_acc, recv_start, part_out), add_rows(ctx_acc, recv_start, part_ctx)), None

    start_sums = (jnp.zeros((NODES, ATT_WIDTH), jnp.float32), jnp.zeros((NODES, HEADS * E), jnp.float32))
    (out_sum, ctx_sum), _ = lax.scan(sum_step, start_sums, slot_ids)
    ctx_heads = ctx_sum.reshape(NODES, HEADS, E)
    edge_value = w_edge_value.astype(jnp.float32).reshape(E, HEADS, HEAD_DIM)
    carried = jnp.einsum("ihe,ehd->ihd", ctx_heads, edge_value, precision=lax.Precision.HIGHEST).reshape(NODES, ATT_WIDTH)
    attended = (out_sum + carried).astype(jnp.bfloat16)
    mixed = (nodes.astype(jnp.float32) + jnp.dot(attended, w_out, preferred_element_type=jnp.float32)).astype(jnp.bfloat16)

    d_att = jnp.dot(d_out, w_out.T, preferred_element_type=jnp.float32).astype(jnp.bfloat16)
    d_att_heads = d_att.astype(jnp.float32).reshape(NODES, HEADS, HEAD_DIM)
    d_ctx = jnp.einsum("ihd,ehd->ihe", d_att_heads, edge_value).astype(jnp.bfloat16)
    d_ctx_f = d_ctx.astype(jnp.float32)
    grad_edge_value = jnp.einsum("ihe,ihd->ehd", ctx_heads, d_att_heads, precision=lax.Precision.HIGHEST).reshape(E, ATT_WIDTH)
    delta = (jnp.sum(d_att_heads * out_sum.reshape(NODES, HEADS, HEAD_DIM), axis=2)
             + jnp.sum(d_ctx_f * ctx_heads, axis=2))

    def grad_step(carry, slot_at):
        grad_query, grad_left, grad_keys, grad_values, grad_right, grad_bias = carry
        recv_block, recv_start, send_start, query_blk, keys_blk, values_blk, pre_act, edge_feat, valid, logits = fetch(slot_at)
        probs = probs_of(logits, valid, recv_block)
        weights = probs.astype(jnp.bfloat16).astype(jnp.float32)
        datt_blk = rows_of(d_att_heads, recv_start)
        dctx_blk = rows_of(d_ctx_f, recv_start)
        delta_blk = rows_of(delta, recv_start)
        edge_f = edge_feat.astype(jnp.float32)
        d_prob = jnp.einsum("ihd,jhd->hij", datt_blk, values_blk) + jnp.einsum("ihe,ije->hij", dctx_blk, edge_f)
        d_logit = jnp.where(valid[None, None, :], probs * (d_prob - delta_blk.T[:, :, None]), 0.0)
        d_logit = d_logit.astype(jnp.bfloat16).astype(jnp.float32)
        part_query = (jnp.einsum("hij,jhd->ihd", d_logit, keys_blk) * scale).reshape(BLK, ATT_WIDTH)
        part_keys = (jnp.einsum("hij,ihd->jhd", d_logit, query_blk) * scale).reshape(BLK, ATT_WIDTH)
        part_values = jnp.einsum("hij,ihd->jhd", weights, datt_blk).reshape(BLK, ATT_WIDTH)
        grad_bias = grad_bias + jnp.einsum("hij,ije->he", d_logit, edge_f)
        d_edge = jnp.einsum("hij,he->ije", d_logit, bias_weight) + jnp.einsum("hij,ihe->ije", weights, dctx_blk)
        sigmoid_v = jax.nn.sigmoid(pre_act)
        d_pre = (d_edge * sigmoid_v * (1.0 + pre_act * (1.0 - sigmoid_v))).astype(jnp.bfloat16).astype(jnp.float32)
        grad_query = add_rows(grad_query, recv_start, part_query)
        grad_left = add_rows(grad_left, recv_start, jnp.sum(d_pre, axis=1))
        grad_keys = add_rows(grad_keys, send_start, part_keys)
        grad_values = add_rows(grad_values, send_start, part_values)
        grad_right = add_rows(grad_right, send_start, jnp.sum(d_pre, axis=0))
        return (grad_query, grad_left, grad_keys, grad_values, grad_right, grad_bias), None

    start_grads = (jnp.zeros((NODES, ATT_WIDTH), jnp.float32), jnp.zeros((NODES, E), jnp.float32),
                   jnp.zeros((NODES, ATT_WIDTH), jnp.float32), jnp.zeros((NODES, ATT_WIDTH), jnp.float32),
                   jnp.zeros((NODES, E), jnp.float32), jnp.zeros((HEADS, E), jnp.float32))
    (grad_query, grad_left, grad_keys, grad_values, grad_right, grad_bias), _ = lax.scan(grad_step, start_grads, slot_ids)
    grad_nodes = (d_out.astype(jnp.float32) + highest(grad_query, w_query) + highest(grad_keys, w_key)
                  + highest(grad_values, w_value) + highest(grad_left, w_left) + highest(grad_right, w_right))
    return mixed, grad_nodes, grad_bias, grad_edge_value
```

```python
import functools

import jax
import jax.numpy as jnp
from jax import lax
from jax.experimental import pallas as pl
from jax.experimental.pallas import tpu as pltpu
from jax.sharding import PartitionSpec as P

NEG_LARGE = -1e30
GROUP = 8
F32 = jnp.float32
BF16 = jnp.bfloat16
VMEM_LIMIT = 60 * 1024 * 1024

RECV_BLOCK, LOCAL_BLOCK, OWNER, IS_LOCAL, SEND_BLOCK, LIVE = range(6)
TOP, TOTAL, DELTA, BLOCK_ID = range(4)


def dot(a, b):
    return jnp.dot(a, b, preferred_element_type=F32)


def dot_t(a, b):
    return lax.dot_general(a, b, (((1,), (1,)), ((), ())), preferred_element_type=F32)


def head_lanes(head_count, att_width, rows):
    lane = lax.broadcasted_iota(jnp.int32, (rows, att_width), 1)
    return lane // (att_width // head_count)


def only_head(x, head_of_lane, head):
    return jnp.where(head_of_lane == head, x, jnp.zeros_like(x))


def first_kernel(
    table, frames_here,
    own, local, got, d_out, frames_send, mask,
    w_query, w_key, w_value, w_left, w_right, w_edge_value, w_out, edge_gain, w_bias,
    probs_out, pair_out, ctx_out, stats_out, att_out, query_out, keys_out, datt_out, left_out, right_out,
    qk_s, dp_s, pair_s,
):
    slot = pl.program_id(0)
    block, att_width = query_out.shape
    heads, edge_width = w_bias.shape
    scale = (att_width // heads) ** (-0.5)
    live = table[slot, LIVE] > 0
    block_id = jnp.full((heads, block), table[slot, RECV_BLOCK], jnp.int32).astype(F32)
    stats_out[BLOCK_ID] = block_id

    @pl.when(jnp.logical_not(live))
    def _():
        stats_out[TOP] = jnp.full((heads, block), NEG_LARGE, F32)
        stats_out[TOTAL] = jnp.zeros((heads, block), F32)
        stats_out[DELTA] = jnp.zeros((heads, block), F32)
        att_out[...] = jnp.zeros_like(att_out)
        ctx_out[...] = jnp.zeros_like(ctx_out)
        datt_out[...] = jnp.zeros_like(datt_out)

    @pl.when(live)
    def _():
        own_x = own[...]
        send_x = jnp.where(table[slot, IS_LOCAL] > 0, local[...].astype(F32), got[...].astype(F32)).astype(BF16)
        query = dot(own_x, w_query[...]).astype(BF16)
        keys = dot(send_x, w_key[...]).astype(BF16)
        values = dot(send_x, w_value[...]).astype(BF16)
        left = dot(own_x, w_left[...]).astype(BF16).astype(F32) * 0.5
        right = dot(send_x, w_right[...]).astype(BF16).astype(F32) * 0.5
        d_att = dot_t(d_out[...], w_out[...]).astype(BF16)
        query_out[...] = query
        keys_out[...] = keys
        datt_out[...] = d_att
        left_out[...] = left
        right_out[...] = right
        frame_rows = jnp.broadcast_to(frames_send[...].astype(F32), (block, edge_width)).T.astype(jnp.int32)
        right_same = right + edge_gain[...].astype(F32) * 0.5
        head_of_lane = head_lanes(heads, att_width, block)
        bias_row = w_bias[...].astype(F32)
        values_edge = jnp.concatenate([values, w_edge_value[...]], axis=0)
        for h in range(heads):
            qk_s[pl.ds(h, block, stride=heads), :] = dot_t(only_head(query, head_of_lane, h), keys) * scale
            both = dot_t(only_head(d_att, head_of_lane, h), values_edge)
            dp_s[pl.ds(h, block, stride=heads), :] = both[:, :block]
            pair_s[pl.ds(heads + h, block, stride=2 * heads), :] = both[:, block:]
            pair_s[pl.ds(h, block, stride=2 * heads), :] = jnp.broadcast_to(bias_row[h : h + 1], (block, edge_width))
        valid = jnp.broadcast_to(mask[...], (heads, block)) > 0
        lane = lax.broadcasted_iota(jnp.int32, (heads, block), 1)
        first_row = table[slot, RECV_BLOCK] * block

        def group(at, carry):
            tops, totals, deltas = carry
            for pair in range(GROUP // 2):
                edges, pairs_in = [], []
                for k in range(2):
                    i = at * GROUP + 2 * pair + k
                    half = jnp.where(frame_rows == frames_here[first_row + i], right_same, right)
                    half = half + left_out[pl.ds(i, 1), :]
                    edges.append((half * jnp.tanh(half) + half).astype(BF16))
                    row = pl.multiple_of(i * 2 * heads, 2 * heads)
                    pair_row = pair_s[pl.ds(row, 2 * heads), :].astype(BF16)
                    pair_out[pl.ds(row, 2 * heads), :] = pair_row
                    pairs_in.append(pair_row)
                scores = dot_t(jnp.concatenate(pairs_in, axis=0), jnp.concatenate(edges, axis=0))
                soft = []
                for k in range(2):
                    i = at * GROUP + 2 * pair + k
                    row = pl.multiple_of(i * heads, heads)
                    top_at, col = 2 * heads * k, block * k
                    logits = qk_s[pl.ds(row, heads), :] + scores[top_at : top_at + heads, col : col + block]
                    d_prob = dp_s[pl.ds(row, heads), :] + scores[top_at + heads : top_at + 2 * heads, col : col + block]
                    logits = jnp.where(valid, logits, NEG_LARGE)
                    top = jnp.max(logits, axis=1, keepdims=True)
                    probs = jnp.exp(logits - top)
                    total = jnp.sum(probs, axis=1, keepdims=True)
                    probs = probs / total
                    delta = jnp.sum(probs * d_prob, axis=1, keepdims=True)
                    centred = probs * (d_prob - delta)
                    both = jnp.concatenate([probs, centred], axis=0)
                    probs_out[pl.ds(pl.multiple_of(i * 2 * heads, 2 * heads), 2 * heads), :] = both
                    soft.append(both.astype(BF16))
                    here = lane == i
                    tops = jnp.where(here, top, tops)
                    totals = jnp.where(here, total, totals)
                    deltas = jnp.where(here, delta, deltas)
                sums = dot(jnp.concatenate(soft, axis=0), jnp.concatenate(edges, axis=1))
                for k in range(2):
                    i = at * GROUP + 2 * pair + k
                    top_at, col = 2 * heads * k, edge_width * k
                    ctx_out[pl.ds(pl.multiple_of(i * 2 * heads, 2 * heads), 2 * heads), :] = (
                        sums[top_at : top_at + 2 * heads, col : col + edge_width]
                    )
            return tops, totals, deltas

        zero = jnp.zeros((heads, block), F32)
        tops, totals, deltas = lax.fori_loop(0, block // GROUP, group, (zero, zero, zero))
        stats_out[TOP] = tops
        stats_out[TOTAL] = totals
        stats_out[DELTA] = deltas
        att = jnp.zeros((block, att_width), F32)
        for h in range(heads):
            probs_h = probs_out[pl.ds(h, block, stride=2 * heads), :].astype(BF16)
            ctx_h = ctx_out[pl.ds(h, block, stride=2 * heads), :].astype(BF16)
            att += dot(probs_h, only_head(values, head_of_lane, h))
            att += dot(ctx_h, only_head(w_edge_value[...], head_of_lane, h))
        att_out[...] = att


def shares(stats_all, stats_mine):
    count = stats_all.shape[0]
    mine = stats_mine[BLOCK_ID]
    top = jnp.full_like(mine, NEG_LARGE)
    for q in range(count):
        top = jnp.maximum(top, jnp.where(stats_all[q, BLOCK_ID] == mine, stats_all[q, TOP], NEG_LARGE))
    total = jnp.zeros_like(mine)
    delta = jnp.zeros_like(mine)
    for q in range(count):
        part = jnp.where(
            stats_all[q, BLOCK_ID] == mine, stats_all[q, TOTAL] * jnp.exp(stats_all[q, TOP] - top), 0.0
        )
        total += part
        delta += part * stats_all[q, DELTA]
    share = stats_mine[TOTAL] * jnp.exp(stats_mine[TOP] - top) / total
    return share, stats_mine[DELTA] - delta / total


def mid_kernel(
    table, stats_all, stats_mine, ctx, att, d_att,
    share_out, shift_out, message,
    att_s, edge_s, bias_s,
):
    slot = pl.program_id(0)
    block, att_width = att.shape
    heads = stats_mine.shape[1]
    edge_width = ctx.shape[1]

    @pl.when(slot == 0)
    def _():
        att_s[...] = jnp.zeros_like(att_s)
        edge_s[...] = jnp.zeros_like(edge_s)
        bias_s[...] = jnp.zeros_like(bias_s)

    share, shift = shares(stats_all, stats_mine)
    share_out[...] = share
    shift_out[...] = shift

    @pl.when(table[slot, LIVE] > 0)
    def _():
        spread = (
            head_lanes(heads, att_width, heads) == lax.broadcasted_iota(jnp.int32, (heads, att_width), 0)
        ).astype(F32)
        share_rows = lax.dot_general(
            share, spread, (((0,), (0,)), ((), ())), preferred_element_type=F32, precision=lax.Precision.HIGHEST
        )
        first_row = pl.multiple_of(table[slot, RECV_BLOCK] * block, block)
        att_s[pl.ds(first_row, block), :] += att[...] * share_rows
        scaled = (d_att[...].astype(F32) * share_rows).astype(BF16)
        weights = jnp.concatenate([share, share * shift], axis=0).astype(BF16)
        head_of_lane = head_lanes(heads, att_width, block)
        head_of_row = lax.broadcasted_iota(jnp.int32, (heads, edge_width), 0)
        edge = jnp.zeros((edge_width, att_width), F32)
        bias = jnp.zeros((heads, edge_width), F32)
        for h in range(heads):
            ctx_h = ctx[pl.ds(h, block, stride=2 * heads), :]
            moved_h = ctx[pl.ds(heads + h, block, stride=2 * heads), :].astype(BF16)
            edge += dot(ctx_h.T.astype(BF16), only_head(scaled, head_of_lane, h))
            sums = dot(weights, jnp.concatenate([ctx_h.astype(BF16), moved_h], axis=1))
            bias += jnp.where(head_of_row == h, sums[:heads, edge_width:] + sums[heads:, :edge_width], 0.0)
        edge_s[...] += edge
        bias_s[...] += bias

    @pl.when(slot == pl.num_programs(0) - 1)
    def _():
        n_send = message.shape[0]
        rows = att_s.shape[0] // n_send
        edge_rows = edge_width // n_send
        for s in range(n_send):
            message[s, 0:rows, :] = att_s[s * rows : (s + 1) * rows, :].astype(BF16)
            message[s, rows : rows + edge_rows, :] = edge_s[s * edge_rows : (s + 1) * edge_rows, :].astype(BF16)
            message[s, rows + edge_rows :, :] = jnp.concatenate([bias_s[...]] * (att_width // edge_width), axis=1).astype(BF16)


def grad_kernel(
    table, frames_here,
    share_in, shift_in, probs_in, pair_in, query_in, keys_in, datt_in, left_in, right_in, frames_send,
    w_query, w_key, w_value, w_left, w_right, edge_gain,
    recv_out, send_out,
    rows_s, diag_s, d_edge_s, right_s, same_s, frame_s, grad_right_s, grad_left_s,
):
    slot = pl.program_id(0)
    block, att_width = query_in.shape
    heads = share_in.shape[0]
    edge_width = w_left.shape[1]
    scale = (att_width // heads) ** (-0.5)
    live = table[slot, LIVE] > 0
    tiles = block // 8
    both_heads = 2 * heads

    @pl.when(slot == 0)
    def _():
        diag_s[...] = jnp.zeros_like(diag_s)

    @pl.when(jnp.logical_not(live))
    def _():
        recv_out[...] = jnp.zeros_like(recv_out)
        send_out[...] = jnp.zeros_like(send_out)

    @pl.when(live)
    def _():
        share, shift = share_in[...], shift_in[...]
        right_s[...] = right_in[...]
        same_s[...] = right_in[...] + edge_gain[...].astype(F32) * 0.5
        frame_s[...] = jnp.broadcast_to(frames_send[...].astype(F32), (block, edge_width)).T.astype(jnp.int32)
        grad_right_s[...] = jnp.zeros_like(grad_right_s)
        lane = lax.broadcasted_iota(jnp.int32, (heads, block), 1)
        first_row = table[slot, RECV_BLOCK] * block

        def group(at, carry):
            for k in range(GROUP):
                i = at * GROUP + k
                here = lane == i
                factor = jnp.sum(jnp.where(here, share, 0.0), axis=1, keepdims=True)
                moved = jnp.sum(jnp.where(here, shift, 0.0), axis=1, keepdims=True)
                row = pl.multiple_of(i * both_heads, both_heads)
                probs = probs_in[pl.ds(row, heads), :]
                centred = probs_in[pl.ds(row + heads, heads), :]
                rows_s[pl.ds(row, heads), :] = (centred + moved * probs) * factor
                rows_s[pl.ds(row + heads, heads), :] = probs * factor
                diag_s[both_heads * k : both_heads * (k + 1), edge_width * k : edge_width * (k + 1)] = (
                    pair_in[pl.ds(row, both_heads), :]
                )
            first = pl.multiple_of(at * GROUP * both_heads, GROUP * both_heads)
            across = rows_s[pl.ds(first, GROUP * both_heads), :].T.astype(BF16)
            d_edge_s[...] = dot(across, diag_s[...])
            frame_of = [frames_here[first_row + at * GROUP + k] for k in range(GROUP)]
            left_of = [
                jnp.broadcast_to(left_in[pl.ds(at * GROUP + k, 1), :], (8, edge_width)) for k in range(GROUP)
            ]
            left_sums = [jnp.zeros((8, edge_width), F32) for _ in range(GROUP)]
            for tile in range(tiles):
                span = slice(8 * tile, 8 * tile + 8)
                right_t, same_t, frame_t = right_s[span, :], same_s[span, :], frame_s[span, :]
                right_sum = grad_right_s[span, :]
                for k in range(GROUP):
                    half = jnp.where(frame_t == frame_of[k], same_t, right_t) + left_of[k]
                    tanh = jnp.tanh(half)
                    slope = (1.0 + tanh) * (half - half * tanh + 1.0)
                    d_pre = slope * d_edge_s[span, edge_width * k : edge_width * (k + 1)]
                    right_sum = right_sum + d_pre
                    left_sums[k] = left_sums[k] + d_pre
                grad_right_s[span, :] = right_sum
            for k in range(GROUP):
                grad_left_s[pl.ds(at * GROUP + k, 1), :] = jnp.sum(left_sums[k], axis=0, keepdims=True)
            return carry

        lax.fori_loop(0, block // GROUP, group, 0)
        query, keys, d_att = query_in[...], keys_in[...], datt_in[...]
        head_of_lane = head_lanes(heads, att_width, block)
        grad_query = jnp.zeros((block, att_width), F32)
        grad_keys = jnp.zeros((block, att_width), F32)
        grad_values = jnp.zeros((block, att_width), F32)
        for h in range(heads):
            d_logit = rows_s[pl.ds(h, block, stride=both_heads), :]
            weight = rows_s[pl.ds(heads + h, block, stride=both_heads), :]
            grad_query += dot(d_logit.astype(BF16), only_head(keys, head_of_lane, h))
            grad_keys += dot(d_logit.T.astype(BF16), only_head(query, head_of_lane, h))
            grad_values += dot(weight.T.astype(BF16), only_head(d_att, head_of_lane, h))
        recv_out[...] = dot_t((grad_query * scale).astype(BF16), w_query[...]) + dot_t(
            (grad_left_s[...] * 0.5).astype(BF16), w_left[...]
        )
        send_out[...] = (
            dot_t((grad_keys * scale).astype(BF16), w_key[...])
            + dot_t(grad_values.astype(BF16), w_value[...])
            + dot_t((grad_right_s[...] * 0.5).astype(BF16), w_right[...])
        ).astype(BF16)


def pack_kernel(slot_of_owner, send_part, early, nodes_piece, w_out, message, mixed_piece):
    n_recv, _, att_width = message.shape
    block = send_part.shape[1]
    rows = nodes_piece.shape[0]
    total = early[0].astype(F32)
    for s in range(1, early.shape[0]):
        total += early[s].astype(F32)
    attended = total[:rows].astype(BF16)
    mixed_piece[...] = (nodes_piece[...].astype(F32) + dot(attended, w_out[...])).astype(BF16)
    extra = total[rows:].astype(BF16)

    for r in range(n_recv):
        slot = slot_of_owner[r]

        @pl.when(slot >= 0)
        def _():
            message[r, :block, :] = send_part[jnp.maximum(slot, 0)]

        @pl.when(slot < 0)
        def _():
            message[r, :block, :] = jnp.zeros((block, att_width), BF16)

        message[r, block:, :] = extra


def merge_kernel(
    table, requested, back, recv_part, send_part, mixed_piece, message, bias_out, acc_s
):
    n_recv, _, att_width = back.shape
    slots, block, _ = recv_part.shape
    n_send = message.shape[0]
    rows = mixed_piece.shape[0]
    acc_s[...] = jnp.zeros_like(acc_s)
    for p in range(slots):
        at = pl.multiple_of(table[p, RECV_BLOCK] * block, block)
        acc_s[pl.ds(at, block), :] += recv_part[p]

        @pl.when(table[p, IS_LOCAL] > 0)
        def _():
            to = pl.multiple_of(table[p, LOCAL_BLOCK] * block, block)
            acc_s[pl.ds(to, block), :] += send_part[p].astype(F32)

    extra = jnp.zeros((back.shape[1] - block, att_width), F32)
    for r in range(n_recv):
        extra += back[r, block:, :].astype(F32)

        @pl.when(requested[r] > 0)
        def _():
            to = pl.multiple_of((requested[r] - 1) * block, block)
            acc_s[pl.ds(to, block), :] += back[r, :block, :].astype(F32)

    edge_rows = message.shape[1] - 2 * rows
    for s in range(n_send):
        message[s, :rows, :] = acc_s[s * rows : (s + 1) * rows, :].astype(BF16)
        message[s, rows : 2 * rows, :] = mixed_piece[...]
        message[s, 2 * rows :, :] = extra[:edge_rows].astype(BF16)
    bias_out[...] = extra[edge_rows:, : bias_out.shape[1]]


def last_kernel(parts, d_out_piece, grad_piece):
    rows = d_out_piece.shape[0]
    total = d_out_piece[...].astype(F32)
    for s in range(parts.shape[0]):
        total += parts[s, :rows, :].astype(F32)
    out = total.astype(grad_piece.dtype)
    for s in range(grad_piece.shape[0]):
        grad_piece[s] = out


def params():
    return pltpu.CompilerParams(vmem_limit_bytes=VMEM_LIMIT)


def whole(*shape):
    return pl.BlockSpec(shape, lambda *_: (0,) * len(shape))


def body(
    nodes,
    frames,
    pairs,
    masks,
    d_out,
    w_query,
    w_key,
    w_value,
    w_left,
    w_right,
    frame_edge,
    w_bias,
    w_edge_value,
    w_out,
):
    rows, width = nodes.shape
    slots, block = masks.shape
    nb_local = rows // block
    heads, edge_width = w_bias.shape
    att_width = w_query.shape[1]
    my_recv = lax.axis_index("recv")
    my_send = lax.axis_index("send")
    n_recv = lax.axis_size("recv")
    n_send = lax.axis_size("send")
    base_block = my_recv * nb_local
    piece = rows // n_send
    edge_piece = edge_width // n_send

    recv_blocks, send_blocks = pairs[0], pairs[1]
    owners = send_blocks // nb_local
    is_local = owners == my_recv
    live = jnp.any(masks > 0, axis=1)
    hits = (owners[None, :] == jnp.arange(n_recv, dtype=jnp.int32)[:, None]) & ~is_local[None, :]
    wanted = jnp.sum(jnp.where(hits, (send_blocks % nb_local)[None, :] + 1, 0), axis=1)
    slot_of_owner = jnp.sum(jnp.where(hits, jnp.arange(slots, dtype=jnp.int32)[None, :] + 1, 0), axis=1) - 1
    requested = lax.all_to_all(wanted, "recv", split_axis=0, concat_axis=0, tiled=True)
    table = jnp.stack(
        [
            recv_blocks - base_block,
            jnp.where(is_local, send_blocks - base_block, 0),
            jnp.where(is_local, 0, owners),
            is_local.astype(jnp.int32),
            send_blocks,
            live.astype(jnp.int32),
        ],
        axis=1,
    )
    node_blocks = nodes.reshape(nb_local, block, width)
    replies = jnp.take(node_blocks, jnp.maximum(requested - 1, 0), axis=0)
    got = lax.all_to_all(replies, "recv", split_axis=0, concat_axis=0, tiled=True)

    frames_here = lax.dynamic_slice_in_dim(frames, my_recv * rows, rows)
    frame_rows = frames.reshape(frames.shape[0] // block, 1, block)
    gain = frame_edge.reshape(1, edge_width)
    d_out_blocks = d_out.reshape(nb_local, block, width)

    def per_slot(*shape):
        return pl.BlockSpec((None, *shape), lambda p, *_: (p,) + (0,) * len(shape))

    def shape_of(dtype, *shape):
        return jax.ShapeDtypeStruct((slots, *shape), dtype)

    both = 2 * heads
    outs = (
        (F32, block * both, block),
        (BF16, block * both, edge_width),
        (F32, block * both, edge_width),
        (F32, 4, heads, block),
        (F32, block, att_width),
        (BF16, block, att_width),
        (BF16, block, att_width),
        (BF16, block, att_width),
        (F32, block, edge_width),
        (F32, block, edge_width),
    )
    own_spec = pl.BlockSpec((None, block, width), lambda p, t, f: (t[p, RECV_BLOCK], 0, 0))
    frame_spec = pl.BlockSpec((None, 1, block), lambda p, t, f: (t[p, SEND_BLOCK], 0, 0))
    probs, pair_rows, ctx, stats, att, query, keys, d_att, left, right = pl.pallas_call(
        first_kernel,
        out_shape=tuple(shape_of(*o) for o in outs),
        grid_spec=pltpu.PrefetchScalarGridSpec(
            num_scalar_prefetch=2,
            grid=(slots,),
            in_specs=[
                own_spec,
                pl.BlockSpec((None, block, width), lambda p, t, f: (t[p, LOCAL_BLOCK], 0, 0)),
                pl.BlockSpec((None, block, width), lambda p, t, f: (t[p, OWNER], 0, 0)),
                own_spec,
                frame_spec,
                per_slot(1, block),
                whole(width, att_width),
                whole(width, att_width),
                whole(width, att_width),
                whole(width, edge_width),
                whole(width, edge_width),
                whole(edge_width, att_width),
                whole(att_width, width),
                whole(1, edge_width),
                whole(heads, edge_width),
            ],
            out_specs=[per_slot(*o[1:]) for o in outs],
            scratch_shapes=[
                pltpu.VMEM((block * heads, block), F32),
                pltpu.VMEM((block * heads, block), F32),
                pltpu.VMEM((block * both, edge_width), F32),
            ],
        ),
        compiler_params=params(),
        name="first",
    )(
        table, frames_here, node_blocks, node_blocks, got, d_out_blocks, frame_rows,
        masks.reshape(slots, 1, block), w_query, w_key, w_value, w_left, w_right,
        w_edge_value, w_out, gain, w_bias,
    )

    stats_all = lax.all_gather(stats, "send", axis=0, tiled=True)
    early_rows = piece + edge_piece + heads
    share, shift, early_out = pl.pallas_call(
        mid_kernel,
        out_shape=(
            shape_of(F32, heads, block),
            shape_of(F32, heads, block),
            jax.ShapeDtypeStruct((n_send, early_rows, att_width), BF16),
        ),
        grid_spec=pltpu.PrefetchScalarGridSpec(
            num_scalar_prefetch=1,
            grid=(slots,),
            in_specs=[
                whole(slots * n_send, 4, heads, block),
                per_slot(4, heads, block),
                per_slot(block * both, edge_width),
                per_slot(block, att_width),
                per_slot(block, att_width),
            ],
            out_specs=[
                per_slot(heads, block),
                per_slot(heads, block),
                whole(n_send, early_rows, att_width),
            ],
            scratch_shapes=[
                pltpu.VMEM((rows, att_width), F32),
                pltpu.VMEM((edge_width, att_width), F32),
                pltpu.VMEM((heads, edge_width), F32),
            ],
        ),
        compiler_params=params(),
        name="mid",
    )(table, stats_all, stats, ctx, att, d_att)
    early = lax.all_to_all(early_out, "send", split_axis=0, concat_axis=0, tiled=True)

    recv_part, send_part = pl.pallas_call(
        grad_kernel,
        out_shape=(shape_of(F32, block, att_width), shape_of(BF16, block, att_width)),
        grid_spec=pltpu.PrefetchScalarGridSpec(
            num_scalar_prefetch=2,
            grid=(slots,),
            in_specs=[
                per_slot(heads, block),
                per_slot(heads, block),
                per_slot(block * both, block),
                per_slot(block * both, edge_width),
                per_slot(block, att_width),
                per_slot(block, att_width),
                per_slot(block, att_width),
                per_slot(block, edge_width),
                per_slot(block, edge_width),
                frame_spec,
                whole(width, att_width),
                whole(width, att_width),
                whole(width, att_width),
                whole(width, edge_width),
                whole(width, edge_width),
                whole(1, edge_width),
            ],
            out_specs=[per_slot(block, att_width), per_slot(block, att_width)],
            scratch_shapes=[
                pltpu.VMEM((block * both, block), F32),
                pltpu.VMEM((GROUP * both, GROUP * edge_width), BF16),
                pltpu.VMEM((block, GROUP * edge_width), F32),
                pltpu.VMEM((block, edge_width), F32),
                pltpu.VMEM((block, edge_width), F32),
                pltpu.VMEM((block, edge_width), jnp.int32),
                pltpu.VMEM((block, edge_width), F32),
                pltpu.VMEM((block, edge_width), F32),
            ],
        ),
        compiler_params=params(),
        cost_estimate=pl.CostEstimate(flops=40_000_000_000, bytes_accessed=12_000_000, transcendentals=8_000_000),
        name="grad",
    )(
        table, frames_here, share, shift, probs, pair_rows, query, keys, d_att, left, right, frame_rows,
        w_query, w_key, w_value, w_left, w_right, gain,
    )

    nodes_piece = lax.dynamic_slice_in_dim(nodes, my_send * piece, piece)
    d_out_piece = lax.dynamic_slice_in_dim(d_out, my_send * piece, piece)
    smem = pl.BlockSpec(memory_space=pltpu.SMEM)
    vmem = pl.BlockSpec(memory_space=pltpu.VMEM)
    message, mixed_piece = pl.pallas_call(
        pack_kernel,
        out_shape=(
            jax.ShapeDtypeStruct((n_recv, block + edge_piece + heads, att_width), BF16),
            jax.ShapeDtypeStruct((piece, width), BF16),
        ),
        in_specs=[smem, vmem, vmem, vmem, vmem],
        out_specs=(vmem, vmem),
        compiler_params=params(),
        name="pack",
    )(slot_of_owner, send_part, early, nodes_piece, w_out)
    back = lax.all_to_all(message, "recv", split_axis=0, concat_axis=0, tiled=True)
    message, grad_bias = pl.pallas_call(
        merge_kernel,
        out_shape=(
            jax.ShapeDtypeStruct((n_send, 2 * piece + edge_piece, att_width), BF16),
            jax.ShapeDtypeStruct((heads, edge_width), F32),
        ),
        in_specs=[smem, smem, vmem, vmem, vmem, vmem],
        out_specs=(vmem, vmem),
        scratch_shapes=[pltpu.VMEM((rows, att_width), F32)],
        compiler_params=params(),
        name="merge",
    )(table, requested, back, recv_part, send_part, mixed_piece)
    parts = lax.all_to_all(message, "send", split_axis=0, concat_axis=0, tiled=True)
    grad_out = pl.pallas_call(
        last_kernel,
        out_shape=jax.ShapeDtypeStruct((n_send, piece, width), BF16),
        in_specs=[vmem, vmem],
        out_specs=vmem,
        compiler_params=params(),
        name="last",
    )(parts, d_out_piece)
    grad_nodes = lax.all_to_all(grad_out, "send", split_axis=0, concat_axis=0, tiled=True)
    mixed = parts[:, piece : 2 * piece].reshape(rows, width)
    grad_edge_value = parts[:, 2 * piece :].reshape(edge_width, att_width).astype(F32)
    return (mixed, grad_nodes.reshape(rows, width).astype(F32), grad_bias, grad_edge_value)


def solution(mesh):
    in_specs = (
        P("recv", None),
        P(),
        P(None, ("recv", "send")),
        P(("recv", "send"), None),
        P("recv", None),
        P(),
        P(),
        P(),
        P(),
        P(),
        P(),
        P(),
        P(),
        P(),
    )
    out_specs = (P("recv", None), P("recv", None), P(), P())
    return jax.shard_map(body, mesh=mesh, in_specs=in_specs, out_specs=out_specs, check_vma=False)
```

```python
import functools

import jax
import jax.numpy as jnp
from jax import lax
from jax.experimental import pallas as pl
from jax.experimental.pallas import tpu as pltpu
from jax.sharding import PartitionSpec as P

NEG_LARGE = -1e30
GROUP = 8
F32 = jnp.float32
BF16 = jnp.bfloat16
VMEM_LIMIT = 60 * 1024 * 1024

RECV_BLOCK, LOCAL_BLOCK, OWNER, IS_LOCAL, SEND_BLOCK, LIVE = range(6)
TOP, TOTAL, DELTA, BLOCK_ID = range(4)


def dot(a, b):
    return jnp.dot(a, b, preferred_element_type=F32)


def dot_t(a, b):
    return lax.dot_general(a, b, (((1,), (1,)), ((), ())), preferred_element_type=F32)


def head_lanes(head_count, att_width, rows):
    lane = lax.broadcasted_iota(jnp.int32, (rows, att_width), 1)
    return lane // (att_width // head_count)


def only_head(x, head_of_lane, head):
    return jnp.where(head_of_lane == head, x, jnp.zeros_like(x))


def first_kernel(
    table, frames_here,
    own, local, got, d_out, frames_send, mask,
    w_query, w_key, w_value, w_left, w_right, w_edge_value, w_out, edge_gain, w_bias,
    probs_out, pair_out, ctx_out, stats_out, att_out, query_out, keys_out, datt_out, left_out, right_out,
    qk_s, dp_s, pair_s, edge_s, score_s,
):
    slot = pl.program_id(0)
    block, att_width = query_out.shape
    heads, edge_width = w_bias.shape
    both_heads = 2 * heads
    scale = (att_width // heads) ** (-0.5)
    live = table[slot, LIVE] > 0
    block_id = jnp.full((heads, block), table[slot, RECV_BLOCK], jnp.int32).astype(F32)
    stats_out[BLOCK_ID] = block_id

    @pl.when(jnp.logical_not(live))
    def _():
        stats_out[TOP] = jnp.full((heads, block), NEG_LARGE, F32)
        stats_out[TOTAL] = jnp.zeros((heads, block), F32)
        stats_out[DELTA] = jnp.zeros((heads, block), F32)
        att_out[...] = jnp.zeros_like(att_out)
        ctx_out[...] = jnp.zeros_like(ctx_out)
        datt_out[...] = jnp.zeros_like(datt_out)

    @pl.when(live)
    def _():
        own_x = own[...]
        send_x = jnp.where(table[slot, IS_LOCAL] > 0, local[...].astype(F32), got[...].astype(F32)).astype(BF16)
        query = dot(own_x, w_query[...]).astype(BF16)
        keys = dot(send_x, w_key[...]).astype(BF16)
        values = dot(send_x, w_value[...]).astype(BF16)
        left = dot(own_x, w_left[...]).astype(BF16).astype(F32) * 0.5
        right = dot(send_x, w_right[...]).astype(BF16).astype(F32) * 0.5
        d_att = dot_t(d_out[...], w_out[...]).astype(BF16)
        query_out[...] = query
        keys_out[...] = keys
        datt_out[...] = d_att
        left_out[...] = left
        right_out[...] = right
        frame_rows = jnp.broadcast_to(frames_send[...].astype(F32), (block, edge_width)).T.astype(jnp.int32)
        right_same = right + edge_gain[...].astype(F32) * 0.5
        head_of_lane = head_lanes(heads, att_width, block)
        bias_row = w_bias[...].astype(F32)
        values_edge = jnp.concatenate([values, w_edge_value[...]], axis=0)
        for h in range(heads):
            qk_s[pl.ds(h, block, stride=heads), :] = dot_t(only_head(query, head_of_lane, h), keys) * scale
            both = dot_t(only_head(d_att, head_of_lane, h), values_edge)
            dp_s[pl.ds(h, block, stride=heads), :] = both[:, :block]
            pair_s[pl.ds(heads + h, block, stride=2 * heads), :] = both[:, block:]
            pair_s[pl.ds(h, block, stride=2 * heads), :] = jnp.broadcast_to(bias_row[h : h + 1], (block, edge_width))
        valid = jnp.broadcast_to(mask[...], (heads, block)) > 0
        lane = lax.broadcasted_iota(jnp.int32, (heads, block), 1)
        first_row = table[slot, RECV_BLOCK] * block

        groups = block // GROUP

        def edge_stage(at):
            for k in range(GROUP):
                i = at * GROUP + k
                half = jnp.where(frame_rows == frames_here[first_row + i], right_same, right)
                half = half + left_out[pl.ds(i, 1), :]
                edge_s[pl.ds(pl.multiple_of(i * block, block), block), :] = (half * jnp.tanh(half) + half).astype(BF16)

        def score_stage(at):
            for pair in range(GROUP // 2):
                i = at * GROUP + 2 * pair
                rows = pl.ds(pl.multiple_of(i * both_heads, 2 * both_heads), 2 * both_heads)
                pair_rows = pair_s[rows, :].astype(BF16)
                pair_out[rows, :] = pair_rows
                scores = dot_t(pair_rows, edge_s[pl.ds(pl.multiple_of(i * block, 2 * block), 2 * block), :])
                for k in range(2):
                    row = pl.multiple_of((i + k) * both_heads, both_heads)
                    score_s[pl.ds(row, both_heads), :] = scores[
                        both_heads * k : both_heads * (k + 1), block * k : block * (k + 1)
                    ]

        def soft_stage(at, carry):
            tops, totals, deltas = carry
            for k in range(GROUP):
                i = at * GROUP + k
                row = pl.multiple_of(i * heads, heads)
                both_row = pl.multiple_of(i * both_heads, both_heads)
                logits = qk_s[pl.ds(row, heads), :] + score_s[pl.ds(both_row, heads), :]
                d_prob = dp_s[pl.ds(row, heads), :] + score_s[pl.ds(both_row + heads, heads), :]
                logits = jnp.where(valid, logits, NEG_LARGE)
                top = jnp.max(logits, axis=1, keepdims=True)
                probs = jnp.exp(logits - top)
                total = jnp.sum(probs, axis=1, keepdims=True)
                probs = probs * (1.0 / total)
                delta = jnp.sum(probs * d_prob, axis=1, keepdims=True)
                probs_out[pl.ds(both_row, heads), :] = probs
                probs_out[pl.ds(both_row + heads, heads), :] = probs * (d_prob - delta)
                here = lane == i
                tops = jnp.where(here, top, tops)
                totals = jnp.where(here, total, totals)
                deltas = jnp.where(here, delta, deltas)
            return tops, totals, deltas

        def ctx_stage(at):
            for pair in range(GROUP // 2):
                i = at * GROUP + 2 * pair
                rows = pl.ds(pl.multiple_of(i * both_heads, 2 * both_heads), 2 * both_heads)
                edges = edge_s[pl.ds(pl.multiple_of(i * block, 2 * block), 2 * block), :]
                sums = dot(probs_out[rows, :].astype(BF16), jnp.concatenate([edges[:block], edges[block:]], axis=1))
                for k in range(2):
                    row = pl.multiple_of((i + k) * both_heads, both_heads)
                    ctx_out[pl.ds(row, both_heads), :] = sums[
                        both_heads * k : both_heads * (k + 1), edge_width * k : edge_width * (k + 1)
                    ]

        def step(at, carry):
            def clamp(x):
                return jnp.clip(x, 0, groups - 1)

            ctx_stage(clamp(at - 3))
            carry = soft_stage(clamp(at - 2), carry)
            score_stage(clamp(at - 1))
            edge_stage(clamp(at))
            return carry

        zero = jnp.zeros((heads, block), F32)
        tops, totals, deltas = lax.fori_loop(0, groups + 3, step, (zero, zero, zero))
        stats_out[TOP] = tops
        stats_out[TOTAL] = totals
        stats_out[DELTA] = deltas
        att = jnp.zeros((block, att_width), F32)
        for h in range(heads):
            probs_h = probs_out[pl.ds(h, block, stride=2 * heads), :].astype(BF16)
            ctx_h = ctx_out[pl.ds(h, block, stride=2 * heads), :].astype(BF16)
            att += dot(probs_h, only_head(values, head_of_lane, h))
            att += dot(ctx_h, only_head(w_edge_value[...], head_of_lane, h))
        att_out[...] = att


def shares(stats_all, stats_mine):
    count = stats_all.shape[0]
    mine = stats_mine[BLOCK_ID]
    top = jnp.full_like(mine, NEG_LARGE)
    for q in range(count):
        top = jnp.maximum(top, jnp.where(stats_all[q, BLOCK_ID] == mine, stats_all[q, TOP], NEG_LARGE))
    total = jnp.zeros_like(mine)
    delta = jnp.zeros_like(mine)
    for q in range(count):
        part = jnp.where(
            stats_all[q, BLOCK_ID] == mine, stats_all[q, TOTAL] * jnp.exp(stats_all[q, TOP] - top), 0.0
        )
        total += part
        delta += part * stats_all[q, DELTA]
    share = stats_mine[TOTAL] * jnp.exp(stats_mine[TOP] - top) / total
    return share, stats_mine[DELTA] - delta / total


def mid_kernel(
    table, stats_all, stats_mine, ctx, att, d_att,
    share_out, shift_out, message,
    att_s, edge_s, bias_s,
):
    slot = pl.program_id(0)
    block, att_width = att.shape
    heads = stats_mine.shape[1]
    edge_width = ctx.shape[1]

    @pl.when(slot == 0)
    def _():
        att_s[...] = jnp.zeros_like(att_s)
        edge_s[...] = jnp.zeros_like(edge_s)
        bias_s[...] = jnp.zeros_like(bias_s)

    share, shift = shares(stats_all, stats_mine)
    share_out[...] = share
    shift_out[...] = shift

    @pl.when(table[slot, LIVE] > 0)
    def _():
        spread = (
            head_lanes(heads, att_width, heads) == lax.broadcasted_iota(jnp.int32, (heads, att_width), 0)
        ).astype(F32)
        share_rows = lax.dot_general(
            share, spread, (((0,), (0,)), ((), ())), preferred_element_type=F32, precision=lax.Precision.HIGHEST
        )
        first_row = pl.multiple_of(table[slot, RECV_BLOCK] * block, block)
        att_s[pl.ds(first_row, block), :] += att[...] * share_rows
        scaled = (d_att[...].astype(F32) * share_rows).astype(BF16)
        weights = jnp.concatenate([share, share * shift], axis=0).astype(BF16)
        head_of_lane = head_lanes(heads, att_width, block)
        head_of_row = lax.broadcasted_iota(jnp.int32, (heads, edge_width), 0)
        edge = jnp.zeros((edge_width, att_width), F32)
        bias = jnp.zeros((heads, edge_width), F32)
        for h in range(heads):
            ctx_h = ctx[pl.ds(h, block, stride=2 * heads), :]
            moved_h = ctx[pl.ds(heads + h, block, stride=2 * heads), :].astype(BF16)
            edge += dot(ctx_h.T.astype(BF16), only_head(scaled, head_of_lane, h))
            sums = dot(weights, jnp.concatenate([ctx_h.astype(BF16), moved_h], axis=1))
            bias += jnp.where(head_of_row == h, sums[:heads, edge_width:] + sums[heads:, :edge_width], 0.0)
        edge_s[...] += edge
        bias_s[...] += bias

    @pl.when(slot == pl.num_programs(0) - 1)
    def _():
        n_send = message.shape[0]
        rows = att_s.shape[0] // n_send
        edge_rows = edge_width // n_send
        for s in range(n_send):
            message[s, 0:rows, :] = att_s[s * rows : (s + 1) * rows, :].astype(BF16)
            message[s, rows : rows + edge_rows, :] = edge_s[s * edge_rows : (s + 1) * edge_rows, :].astype(BF16)
            message[s, rows + edge_rows :, :] = jnp.concatenate([bias_s[...]] * (att_width // edge_width), axis=1).astype(BF16)


def grad_kernel(
    table, frames_here,
    share_in, shift_in, probs_in, pair_in, query_in, keys_in, datt_in, left_in, right_in, frames_send,
    w_query, w_key, w_value, w_left, w_right, edge_gain,
    recv_out, send_out,
    rows_s, diag_s, d_edge_s, right_s, same_s, frame_s, grad_right_s, grad_left_s,
):
    slot = pl.program_id(0)
    block, att_width = query_in.shape
    heads = share_in.shape[0]
    edge_width = w_left.shape[1]
    scale = (att_width // heads) ** (-0.5)
    live = table[slot, LIVE] > 0
    tiles = block // 8
    both_heads = 2 * heads

    @pl.when(slot == 0)
    def _():
        diag_s[...] = jnp.zeros_like(diag_s)

    @pl.when(jnp.logical_not(live))
    def _():
        recv_out[...] = jnp.zeros_like(recv_out)
        send_out[...] = jnp.zeros_like(send_out)

    @pl.when(live)
    def _():
        share, shift = share_in[...], shift_in[...]
        right_s[...] = right_in[...]
        same_s[...] = right_in[...] + edge_gain[...].astype(F32) * 0.5
        frame_s[...] = jnp.broadcast_to(frames_send[...].astype(F32), (block, edge_width)).T.astype(jnp.int32)
        grad_right_s[...] = jnp.zeros_like(grad_right_s)
        lane = lax.broadcasted_iota(jnp.int32, (heads, block), 1)
        first_row = table[slot, RECV_BLOCK] * block

        def group(at, carry):
            for k in range(GROUP):
                i = at * GROUP + k
                here = lane == i
                factor = jnp.sum(jnp.where(here, share, 0.0), axis=1, keepdims=True)
                moved = jnp.sum(jnp.where(here, shift, 0.0), axis=1, keepdims=True)
                row = pl.multiple_of(i * both_heads, both_heads)
                probs = probs_in[pl.ds(row, heads), :]
                centred = probs_in[pl.ds(row + heads, heads), :]
                rows_s[pl.ds(row, heads), :] = (centred + moved * probs) * factor
                rows_s[pl.ds(row + heads, heads), :] = probs * factor
                diag_s[both_heads * k : both_heads * (k + 1), edge_width * k : edge_width * (k + 1)] = (
                    pair_in[pl.ds(row, both_heads), :]
                )
            first = pl.multiple_of(at * GROUP * both_heads, GROUP * both_heads)
            across = rows_s[pl.ds(first, GROUP * both_heads), :].T.astype(BF16)
            d_edge_s[...] = dot(across, diag_s[...])
            frame_of = [frames_here[first_row + at * GROUP + k] for k in range(GROUP)]
            left_of = [
                jnp.broadcast_to(left_in[pl.ds(at * GROUP + k, 1), :], (8, edge_width)) for k in range(GROUP)
            ]
            left_sums = [jnp.zeros((8, edge_width), F32) for _ in range(GROUP)]
            for tile in range(tiles):
                span = slice(8 * tile, 8 * tile + 8)
                right_t, same_t, frame_t = right_s[span, :], same_s[span, :], frame_s[span, :]
                right_sum = grad_right_s[span, :]
                for k in range(GROUP):
                    half = jnp.where(frame_t == frame_of[k], same_t, right_t) + left_of[k]
                    tanh = jnp.tanh(half)
                    slope = (1.0 + tanh) * (half - half * tanh + 1.0)
                    d_pre = slope * d_edge_s[span, edge_width * k : edge_width * (k + 1)]
                    right_sum = right_sum + d_pre
                    left_sums[k] = left_sums[k] + d_pre
                grad_right_s[span, :] = right_sum
            for k in range(GROUP):
                grad_left_s[pl.ds(at * GROUP + k, 1), :] = jnp.sum(left_sums[k], axis=0, keepdims=True)
            return carry

        lax.fori_loop(0, block // GROUP, group, 0)
        query, keys, d_att = query_in[...], keys_in[...], datt_in[...]
        head_of_lane = head_lanes(heads, att_width, block)
        grad_query = jnp.zeros((block, att_width), F32)
        grad_keys = jnp.zeros((block, att_width), F32)
        grad_values = jnp.zeros((block, att_width), F32)
        for h in range(heads):
            d_logit = rows_s[pl.ds(h, block, stride=both_heads), :]
            weight = rows_s[pl.ds(heads + h, block, stride=both_heads), :]
            grad_query += dot(d_logit.astype(BF16), only_head(keys, head_of_lane, h))
            grad_keys += dot(d_logit.T.astype(BF16), only_head(query, head_of_lane, h))
            grad_values += dot(weight.T.astype(BF16), only_head(d_att, head_of_lane, h))
        recv_out[...] = dot_t((grad_query * scale).astype(BF16), w_query[...]) + dot_t(
            (grad_left_s[...] * 0.5).astype(BF16), w_left[...]
        )
        send_out[...] = (
            dot_t((grad_keys * scale).astype(BF16), w_key[...])
            + dot_t(grad_values.astype(BF16), w_value[...])
            + dot_t((grad_right_s[...] * 0.5).astype(BF16), w_right[...])
        ).astype(BF16)


def pack_kernel(slot_of_owner, send_part, early, nodes_piece, w_out, message, mixed_piece):
    n_recv, _, att_width = message.shape
    block = send_part.shape[1]
    rows = nodes_piece.shape[0]
    total = early[0].astype(F32)
    for s in range(1, early.shape[0]):
        total += early[s].astype(F32)
    attended = total[:rows].astype(BF16)
    mixed_piece[...] = (nodes_piece[...].astype(F32) + dot(attended, w_out[...])).astype(BF16)
    extra = total[rows:].astype(BF16)

    for r in range(n_recv):
        slot = slot_of_owner[r]

        @pl.when(slot >= 0)
        def _():
            message[r, :block, :] = send_part[jnp.maximum(slot, 0)]

        @pl.when(slot < 0)
        def _():
            message[r, :block, :] = jnp.zeros((block, att_width), BF16)

        message[r, block:, :] = extra


def merge_kernel(
    table, requested, back, recv_part, send_part, mixed_piece, message, bias_out, acc_s
):
    n_recv, _, att_width = back.shape
    slots, block, _ = recv_part.shape
    n_send = message.shape[0]
    rows = mixed_piece.shape[0]
    acc_s[...] = jnp.zeros_like(acc_s)
    for p in range(slots):
        at = pl.multiple_of(table[p, RECV_BLOCK] * block, block)
        acc_s[pl.ds(at, block), :] += recv_part[p]

        @pl.when(table[p, IS_LOCAL] > 0)
        def _():
            to = pl.multiple_of(table[p, LOCAL_BLOCK] * block, block)
            acc_s[pl.ds(to, block), :] += send_part[p].astype(F32)

    extra = jnp.zeros((back.shape[1] - block, att_width), F32)
    for r in range(n_recv):
        extra += back[r, block:, :].astype(F32)

        @pl.when(requested[r] > 0)
        def _():
            to = pl.multiple_of((requested[r] - 1) * block, block)
            acc_s[pl.ds(to, block), :] += back[r, :block, :].astype(F32)

    edge_rows = message.shape[1] - 2 * rows
    for s in range(n_send):
        message[s, :rows, :] = acc_s[s * rows : (s + 1) * rows, :].astype(BF16)
        message[s, rows : 2 * rows, :] = mixed_piece[...]
        message[s, 2 * rows :, :] = extra[:edge_rows].astype(BF16)
    bias_out[...] = extra[edge_rows:, : bias_out.shape[1]]


def last_kernel(parts, d_out_piece, grad_piece):
    rows = d_out_piece.shape[0]
    total = d_out_piece[...].astype(F32)
    for s in range(parts.shape[0]):
        total += parts[s, :rows, :].astype(F32)
    out = total.astype(grad_piece.dtype)
    for s in range(grad_piece.shape[0]):
        grad_piece[s] = out


def params():
    return pltpu.CompilerParams(vmem_limit_bytes=VMEM_LIMIT)


def whole(*shape):
    return pl.BlockSpec(shape, lambda *_: (0,) * len(shape))


def body(
    nodes,
    frames,
    pairs,
    masks,
    d_out,
    w_query,
    w_key,
    w_value,
    w_left,
    w_right,
    frame_edge,
    w_bias,
    w_edge_value,
    w_out,
):
    rows, width = nodes.shape
    slots, block = masks.shape
    nb_local = rows // block
    heads, edge_width = w_bias.shape
    att_width = w_query.shape[1]
    my_recv = lax.axis_index("recv")
    my_send = lax.axis_index("send")
    n_recv = lax.axis_size("recv")
    n_send = lax.axis_size("send")
    base_block = my_recv * nb_local
    piece = rows // n_send
    edge_piece = edge_width // n_send

    recv_blocks, send_blocks = pairs[0], pairs[1]
    owners = send_blocks // nb_local
    is_local = owners == my_recv
    live = jnp.any(masks > 0, axis=1)
    hits = (owners[None, :] == jnp.arange(n_recv, dtype=jnp.int32)[:, None]) & ~is_local[None, :]
    wanted = jnp.sum(jnp.where(hits, (send_blocks % nb_local)[None, :] + 1, 0), axis=1)
    slot_of_owner = jnp.sum(jnp.where(hits, jnp.arange(slots, dtype=jnp.int32)[None, :] + 1, 0), axis=1) - 1
    requested = lax.all_to_all(wanted, "recv", split_axis=0, concat_axis=0, tiled=True)
    table = jnp.stack(
        [
            recv_blocks - base_block,
            jnp.where(is_local, send_blocks - base_block, 0),
            jnp.where(is_local, 0, owners),
            is_local.astype(jnp.int32),
            send_blocks,
            live.astype(jnp.int32),
        ],
        axis=1,
    )
    node_blocks = nodes.reshape(nb_local, block, width)
    replies = jnp.take(node_blocks, jnp.maximum(requested - 1, 0), axis=0)
    got = lax.all_to_all(replies, "recv", split_axis=0, concat_axis=0, tiled=True)

    frames_here = lax.dynamic_slice_in_dim(frames, my_recv * rows, rows)
    frame_rows = frames.reshape(frames.shape[0] // block, 1, block)
    gain = frame_edge.reshape(1, edge_width)
    d_out_blocks = d_out.reshape(nb_local, block, width)

    def per_slot(*shape):
        return pl.BlockSpec((None, *shape), lambda p, *_: (p,) + (0,) * len(shape))

    def shape_of(dtype, *shape):
        return jax.ShapeDtypeStruct((slots, *shape), dtype)

    both = 2 * heads
    outs = (
        (F32, block * both, block),
        (BF16, block * both, edge_width),
        (F32, block * both, edge_width),
        (F32, 4, heads, block),
        (F32, block, att_width),
        (BF16, block, att_width),
        (BF16, block, att_width),
        (BF16, block, att_width),
        (F32, block, edge_width),
        (F32, block, edge_width),
    )
    own_spec = pl.BlockSpec((None, block, width), lambda p, t, f: (t[p, RECV_BLOCK], 0, 0))
    frame_spec = pl.BlockSpec((None, 1, block), lambda p, t, f: (t[p, SEND_BLOCK], 0, 0))
    probs, pair_rows, ctx, stats, att, query, keys, d_att, left, right = pl.pallas_call(
        first_kernel,
        out_shape=tuple(shape_of(*o) for o in outs),
        grid_spec=pltpu.PrefetchScalarGridSpec(
            num_scalar_prefetch=2,
            grid=(slots,),
            in_specs=[
                own_spec,
                pl.BlockSpec((None, block, width), lambda p, t, f: (t[p, LOCAL_BLOCK], 0, 0)),
                pl.BlockSpec((None, block, width), lambda p, t, f: (t[p, OWNER], 0, 0)),
                own_spec,
                frame_spec,
                per_slot(1, block),
                whole(width, att_width),
                whole(width, att_width),
                whole(width, att_width),
                whole(width, edge_width),
                whole(width, edge_width),
                whole(edge_width, att_width),
                whole(att_width, width),
                whole(1, edge_width),
                whole(heads, edge_width),
            ],
            out_specs=[per_slot(*o[1:]) for o in outs],
            scratch_shapes=[
                pltpu.VMEM((block * heads, block), F32),
                pltpu.VMEM((block * heads, block), F32),
                pltpu.VMEM((block * both, edge_width), F32),
                pltpu.VMEM((block * block, edge_width), BF16),
                pltpu.VMEM((block * both, block), F32),
            ],
        ),
        compiler_params=params(),
        name="first",
    )(
        table, frames_here, node_blocks, node_blocks, got, d_out_blocks, frame_rows,
        masks.reshape(slots, 1, block), w_query, w_key, w_value, w_left, w_right,
        w_edge_value, w_out, gain, w_bias,
    )

    stats_all = lax.all_gather(stats, "send", axis=0, tiled=True)
    early_rows = piece + edge_piece + heads
    share, shift, early_out = pl.pallas_call(
        mid_kernel,
        out_shape=(
            shape_of(F32, heads, block),
            shape_of(F32, heads, block),
            jax.ShapeDtypeStruct((n_send, early_rows, att_width), BF16),
        ),
        grid_spec=pltpu.PrefetchScalarGridSpec(
            num_scalar_prefetch=1,
            grid=(slots,),
            in_specs=[
                whole(slots * n_send, 4, heads, block),
                per_slot(4, heads, block),
                per_slot(block * both, edge_width),
                per_slot(block, att_width),
                per_slot(block, att_width),
            ],
            out_specs=[
                per_slot(heads, block),
                per_slot(heads, block),
                whole(n_send, early_rows, att_width),
            ],
            scratch_shapes=[
                pltpu.VMEM((rows, att_width), F32),
                pltpu.VMEM((edge_width, att_width), F32),
                pltpu.VMEM((heads, edge_width), F32),
            ],
        ),
        compiler_params=params(),
        name="mid",
    )(table, stats_all, stats, ctx, att, d_att)
    early = lax.all_to_all(early_out, "send", split_axis=0, concat_axis=0, tiled=True)

    recv_part, send_part = pl.pallas_call(
        grad_kernel,
        out_shape=(shape_of(F32, block, att_width), shape_of(BF16, block, att_width)),
        grid_spec=pltpu.PrefetchScalarGridSpec(
            num_scalar_prefetch=2,
            grid=(slots,),
            in_specs=[
                per_slot(heads, block),
                per_slot(heads, block),
                per_slot(block * both, block),
                per_slot(block * both, edge_width),
                per_slot(block, att_width),
                per_slot(block, att_width),
                per_slot(block, att_width),
                per_slot(block, edge_width),
                per_slot(block, edge_width),
                frame_spec,
                whole(width, att_width),
                whole(width, att_width),
                whole(width, att_width),
                whole(width, edge_width),
                whole(width, edge_width),
                whole(1, edge_width),
            ],
            out_specs=[per_slot(block, att_width), per_slot(block, att_width)],
            scratch_shapes=[
                pltpu.VMEM((block * both, block), F32),
                pltpu.VMEM((GROUP * both, GROUP * edge_width), BF16),
                pltpu.VMEM((block, GROUP * edge_width), F32),
                pltpu.VMEM((block, edge_width), F32),
                pltpu.VMEM((block, edge_width), F32),
                pltpu.VMEM((block, edge_width), jnp.int32),
                pltpu.VMEM((block, edge_width), F32),
                pltpu.VMEM((block, edge_width), F32),
            ],
        ),
        compiler_params=params(),
        cost_estimate=pl.CostEstimate(flops=40_000_000_000, bytes_accessed=12_000_000, transcendentals=8_000_000),
        name="grad",
    )(
        table, frames_here, share, shift, probs, pair_rows, query, keys, d_att, left, right, frame_rows,
        w_query, w_key, w_value, w_left, w_right, gain,
    )

    nodes_piece = lax.dynamic_slice_in_dim(nodes, my_send * piece, piece)
    d_out_piece = lax.dynamic_slice_in_dim(d_out, my_send * piece, piece)
    smem = pl.BlockSpec(memory_space=pltpu.SMEM)
    vmem = pl.BlockSpec(memory_space=pltpu.VMEM)
    message, mixed_piece = pl.pallas_call(
        pack_kernel,
        out_shape=(
            jax.ShapeDtypeStruct((n_recv, block + edge_piece + heads, att_width), BF16),
            jax.ShapeDtypeStruct((piece, width), BF16),
        ),
        in_specs=[smem, vmem, vmem, vmem, vmem],
        out_specs=(vmem, vmem),
        compiler_params=params(),
        name="pack",
    )(slot_of_owner, send_part, early, nodes_piece, w_out)
    back = lax.all_to_all(message, "recv", split_axis=0, concat_axis=0, tiled=True)
    message, grad_bias = pl.pallas_call(
        merge_kernel,
        out_shape=(
            jax.ShapeDtypeStruct((n_send, 2 * piece + edge_piece, att_width), BF16),
            jax.ShapeDtypeStruct((heads, edge_width), F32),
        ),
        in_specs=[smem, smem, vmem, vmem, vmem, vmem],
        out_specs=(vmem, vmem),
        scratch_shapes=[pltpu.VMEM((rows, att_width), F32)],
        compiler_params=params(),
        name="merge",
    )(table, requested, back, recv_part, send_part, mixed_piece)
    parts = lax.all_to_all(message, "send", split_axis=0, concat_axis=0, tiled=True)
    grad_out = pl.pallas_call(
        last_kernel,
        out_shape=jax.ShapeDtypeStruct((n_send, piece, width), BF16),
        in_specs=[vmem, vmem],
        out_specs=vmem,
        compiler_params=params(),
        name="last",
    )(parts, d_out_piece)
    grad_nodes = lax.all_to_all(grad_out, "send", split_axis=0, concat_axis=0, tiled=True)
    mixed = parts[:, piece : 2 * piece].reshape(rows, width)
    grad_edge_value = parts[:, 2 * piece :].reshape(edge_width, att_width).astype(F32)
    return (mixed, grad_nodes.reshape(rows, width).astype(F32), grad_bias, grad_edge_value)


def solution(mesh):
    in_specs = (
        P("recv", None),
        P(),
        P(None, ("recv", "send")),
        P(("recv", "send"), None),
        P("recv", None),
        P(),
        P(),
        P(),
        P(),
        P(),
        P(),
        P(),
        P(),
        P(),
    )
    out_specs = (P("recv", None), P("recv", None), P(), P())
    return jax.shard_map(body, mesh=mesh, in_specs=in_specs, out_specs=out_specs, check_vma=False)
```

```python
import functools

import jax
import jax.numpy as jnp
from jax import lax
from jax.experimental import pallas as pl
from jax.experimental.pallas import tpu as pltpu
from jax.sharding import PartitionSpec as P

NEG_LARGE = -1e30
GROUP = 8
FIRST_GROUP = 8
F32 = jnp.float32
BF16 = jnp.bfloat16
VMEM_LIMIT = 60 * 1024 * 1024

RECV_BLOCK, LOCAL_BLOCK, OWNER, IS_LOCAL, SEND_BLOCK, LIVE = range(6)
TOP, TOTAL, DELTA, BLOCK_ID = range(4)


def dot(a, b):
    return jnp.dot(a, b, preferred_element_type=F32)


def dot_t(a, b):
    return lax.dot_general(a, b, (((1,), (1,)), ((), ())), preferred_element_type=F32)


def head_lanes(head_count, att_width, rows):
    lane = lax.broadcasted_iota(jnp.int32, (rows, att_width), 1)
    return lane // (att_width // head_count)


def only_head(x, head_of_lane, head):
    return jnp.where(head_of_lane == head, x, jnp.zeros_like(x))


def fill_bases(base_s, frames_here, first_row, frames_send, right, edge_gain):
    block, edge_width = right.shape
    frame_rows = jnp.broadcast_to(frames_send[...].astype(F32), (block, edge_width)).T.astype(jnp.int32)
    same = right + edge_gain[...].astype(F32) * 0.5
    first_frame = frames_here[first_row]

    def fill(at, carry):
        base_s[pl.ds(pl.multiple_of(at * block, block), block), :] = jnp.where(frame_rows == first_frame + at, same, right)
        return carry

    lax.fori_loop(0, frames_here[first_row + block - 1] - first_frame + 1, fill, 0)
    return first_frame


def first_kernel(
    table, frames_here,
    own, local, got, d_out, frames_send, mask,
    w_query, w_key, w_value, w_left, w_right, w_edge_value, w_out, edge_gain, w_bias,
    probs_out, pair_out, ctx_out, stats_out, att_out, query_out, keys_out, datt_out, left_out, right_out,
    qk_s, dp_s, dctx_s, query_s, datt_s, stack_s, edge_s, score_s, base_s,
):
    slot = pl.program_id(0)
    block, att_width = query_out.shape
    heads, edge_width = w_bias.shape
    both_heads = 2 * heads
    scale = (att_width // heads) ** (-0.5)
    live = table[slot, LIVE] > 0
    block_id = jnp.full((heads, block), table[slot, RECV_BLOCK], jnp.int32).astype(F32)
    stats_out[BLOCK_ID] = block_id

    @pl.when(jnp.logical_not(live))
    def _():
        stats_out[TOP] = jnp.full((heads, block), NEG_LARGE, F32)
        stats_out[TOTAL] = jnp.zeros((heads, block), F32)
        stats_out[DELTA] = jnp.zeros((heads, block), F32)
        att_out[...] = jnp.zeros_like(att_out)
        ctx_out[...] = jnp.zeros_like(ctx_out)
        datt_out[...] = jnp.zeros_like(datt_out)

    @pl.when(live)
    def _():
        own_x = own[...]
        send_x = jnp.where(table[slot, IS_LOCAL] > 0, local[...].astype(F32), got[...].astype(F32)).astype(BF16)
        query = dot(own_x, w_query[...]).astype(BF16)
        keys = dot(send_x, w_key[...]).astype(BF16)
        left_out[...] = dot(own_x, w_left[...]).astype(BF16).astype(F32) * 0.5
        right = dot(send_x, w_right[...]).astype(BF16).astype(F32) * 0.5
        d_att = dot_t(d_out[...], w_out[...]).astype(BF16)
        query_out[...] = query
        keys_out[...] = keys
        datt_out[...] = d_att
        right_out[...] = right
        query_s[...] = query.astype(F32)
        datt_s[...] = d_att.astype(F32)
        stack_s[:block, :] = dot(send_x, w_value[...]).astype(BF16)
        stack_s[block:, :] = w_edge_value[...]
        first_row = table[slot, RECV_BLOCK] * block
        first_frame = fill_bases(base_s, frames_here, first_row, frames_send, right, edge_gain)
        own_head = head_lanes(heads, att_width, heads) == lax.broadcasted_iota(jnp.int32, (heads, att_width), 0)
        bias_rows = w_bias[...].astype(F32)
        valid = jnp.broadcast_to(mask[...], (heads, block)) > 0
        lane = lax.broadcasted_iota(jnp.int32, (heads, block), 1)
        groups = block // FIRST_GROUP

        def by_head(rows_ref, at):
            rows = [
                jnp.where(own_head, jnp.broadcast_to(rows_ref[pl.ds(at * FIRST_GROUP + k, 1), :], own_head.shape), 0.0)
                for k in range(FIRST_GROUP)
            ]
            return jnp.concatenate(rows, axis=0).astype(BF16)

        def edge_stage(at):
            rows = pl.ds(pl.multiple_of(at * FIRST_GROUP * heads, FIRST_GROUP * heads), FIRST_GROUP * heads)
            qk_s[rows, :] = dot_t(by_head(query_s, at), keys_out[...]) * scale
            both = dot_t(by_head(datt_s, at), stack_s[...])
            dp_s[rows, :] = both[:, :block]
            dctx_s[rows, :] = both[:, block:]
            for k in range(FIRST_GROUP):
                i = at * FIRST_GROUP + k
                base_row = pl.multiple_of((frames_here[first_row + i] - first_frame) * block, block)
                half = base_s[pl.ds(base_row, block), :] + left_out[pl.ds(i, 1), :]
                edge_s[pl.ds(pl.multiple_of(i * block, block), block), :] = (half * jnp.tanh(half) + half).astype(BF16)

        def score_stage(at):
            for pair in range(FIRST_GROUP // 2):
                i = at * FIRST_GROUP + 2 * pair
                rows = pl.ds(pl.multiple_of(i * both_heads, 2 * both_heads), 2 * both_heads)
                d_ctx = dctx_s[pl.ds(pl.multiple_of(i * heads, both_heads), both_heads), :]
                pair_rows = jnp.concatenate([bias_rows, d_ctx[:heads], bias_rows, d_ctx[heads:]], axis=0).astype(BF16)
                pair_out[rows, :] = pair_rows
                scores = dot_t(pair_rows, edge_s[pl.ds(pl.multiple_of(i * block, 2 * block), 2 * block), :])
                for k in range(2):
                    row = pl.multiple_of((i + k) * both_heads, both_heads)
                    score_s[pl.ds(row, both_heads), :] = scores[
                        both_heads * k : both_heads * (k + 1), block * k : block * (k + 1)
                    ]

        def soft_stage(at, carry):
            tops, totals, deltas = carry
            for k in range(FIRST_GROUP):
                i = at * FIRST_GROUP + k
                row = pl.multiple_of(i * heads, heads)
                both_row = pl.multiple_of(i * both_heads, both_heads)
                logits = qk_s[pl.ds(row, heads), :] + score_s[pl.ds(both_row, heads), :]
                d_prob = dp_s[pl.ds(row, heads), :] + score_s[pl.ds(both_row + heads, heads), :]
                logits = jnp.where(valid, logits, NEG_LARGE)
                top = jnp.max(logits, axis=1, keepdims=True)
                probs = jnp.exp(logits - top)
                total = jnp.sum(probs, axis=1, keepdims=True)
                delta = jnp.sum(probs * d_prob, axis=1, keepdims=True)
                inverse = 1.0 / total
                probs = probs * inverse
                delta = delta * inverse
                probs_out[pl.ds(both_row, heads), :] = probs
                probs_out[pl.ds(both_row + heads, heads), :] = probs * (d_prob - delta)
                here = lane == i
                tops = jnp.where(here, top, tops)
                totals = jnp.where(here, total, totals)
                deltas = jnp.where(here, delta, deltas)
            return tops, totals, deltas

        def ctx_stage(at):
            for pair in range(FIRST_GROUP // 2):
                i = at * FIRST_GROUP + 2 * pair
                rows = pl.ds(pl.multiple_of(i * both_heads, 2 * both_heads), 2 * both_heads)
                edges = edge_s[pl.ds(pl.multiple_of(i * block, 2 * block), 2 * block), :]
                sums = dot(probs_out[rows, :].astype(BF16), jnp.concatenate([edges[:block], edges[block:]], axis=1))
                for k in range(2):
                    row = pl.multiple_of((i + k) * both_heads, both_heads)
                    ctx_out[pl.ds(row, both_heads), :] = sums[
                        both_heads * k : both_heads * (k + 1), edge_width * k : edge_width * (k + 1)
                    ]

        def step(at, carry):
            def clamp(x):
                return jnp.clip(x, 0, groups - 1)

            ctx_stage(clamp(at - 3))
            carry = soft_stage(clamp(at - 2), carry)
            score_stage(clamp(at - 1))
            edge_stage(clamp(at))
            return carry

        zero = jnp.zeros((heads, block), F32)
        tops, totals, deltas = lax.fori_loop(0, groups + 3, step, (zero, zero, zero))
        stats_out[TOP] = tops
        stats_out[TOTAL] = totals
        stats_out[DELTA] = deltas
        head_of_lane = head_lanes(heads, att_width, block)
        att = jnp.zeros((block, att_width), F32)
        for h in range(heads):
            rows = pl.ds(h, block, stride=both_heads)
            lhs = jnp.concatenate([probs_out[rows, :], ctx_out[rows, :]], axis=1).astype(BF16)
            att = jnp.where(head_of_lane == h, dot(lhs, stack_s[...]), att)
        att_out[...] = att


def shares(stats_all, stats_mine):
    count = stats_all.shape[0]
    mine = stats_mine[BLOCK_ID]
    top = jnp.full_like(mine, NEG_LARGE)
    for q in range(count):
        top = jnp.maximum(top, jnp.where(stats_all[q, BLOCK_ID] == mine, stats_all[q, TOP], NEG_LARGE))
    total = jnp.zeros_like(mine)
    delta = jnp.zeros_like(mine)
    for q in range(count):
        part = jnp.where(
            stats_all[q, BLOCK_ID] == mine, stats_all[q, TOTAL] * jnp.exp(stats_all[q, TOP] - top), 0.0
        )
        total += part
        delta += part * stats_all[q, DELTA]
    share = stats_mine[TOTAL] * jnp.exp(stats_mine[TOP] - top) / total
    return share, stats_mine[DELTA] - delta / total


def mid_kernel(
    table, stats_all, stats_mine, ctx, att, d_att,
    share_out, shift_out, message,
    att_s, edge_s, bias_s,
):
    slot = pl.program_id(0)
    block, att_width = att.shape
    heads = stats_mine.shape[1]
    edge_width = ctx.shape[1]

    @pl.when(slot == 0)
    def _():
        att_s[...] = jnp.zeros_like(att_s)
        edge_s[...] = jnp.zeros_like(edge_s)
        bias_s[...] = jnp.zeros_like(bias_s)

    share, shift = shares(stats_all, stats_mine)
    share_out[...] = share
    shift_out[...] = shift

    @pl.when(table[slot, LIVE] > 0)
    def _():
        spread = (
            head_lanes(heads, att_width, heads) == lax.broadcasted_iota(jnp.int32, (heads, att_width), 0)
        ).astype(F32)
        share_rows = lax.dot_general(
            share, spread, (((0,), (0,)), ((), ())), preferred_element_type=F32, precision=lax.Precision.HIGHEST
        )
        first_row = pl.multiple_of(table[slot, RECV_BLOCK] * block, block)
        att_s[pl.ds(first_row, block), :] += att[...] * share_rows
        scaled = d_att[...].astype(F32) * share_rows
        weights = jnp.concatenate([share, share * shift], axis=0).astype(BF16)
        head_of_row = lax.broadcasted_iota(jnp.int32, (heads, edge_width), 0)
        head_dim = att_width // heads
        scaled_t = scaled.T.astype(BF16)
        edge = []
        bias = jnp.zeros((heads, edge_width), F32)
        for h in range(heads):
            ctx_h = ctx[pl.ds(h, block, stride=2 * heads), :].astype(BF16)
            moved_h = ctx[pl.ds(heads + h, block, stride=2 * heads), :].astype(BF16)
            edge.append(dot(scaled_t[h * head_dim : (h + 1) * head_dim], ctx_h))
            sums = dot(weights, jnp.concatenate([ctx_h, moved_h], axis=1))
            bias += jnp.where(head_of_row == h, sums[:heads, edge_width:] + sums[heads:, :edge_width], 0.0)
        edge = jnp.concatenate(edge, axis=0)
        edge_s[...] += edge
        bias_s[...] += bias

    @pl.when(slot == pl.num_programs(0) - 1)
    def _():
        n_send = message.shape[0]
        rows = att_s.shape[0] // n_send
        edge_rows = edge_width // n_send
        edge_all = edge_s[...].T
        for s in range(n_send):
            message[s, 0:rows, :] = att_s[s * rows : (s + 1) * rows, :].astype(BF16)
            message[s, rows : rows + edge_rows, :] = edge_all[s * edge_rows : (s + 1) * edge_rows, :].astype(BF16)
            message[s, rows + edge_rows :, :] = jnp.concatenate([bias_s[...]] * (att_width // edge_width), axis=1).astype(BF16)


def grad_kernel(
    table, frames_here,
    share_in, shift_in, probs_in, pair_in, query_in, keys_in, datt_in, left_in, right_in, frames_send,
    w_query, w_key, w_value, w_left, w_right, edge_gain,
    recv_out, send_out,
    rows_s, diag_s, even_s, odd_s, base_s, grad_right_s, grad_left_s,
):
    slot = pl.program_id(0)
    block, att_width = query_in.shape
    heads = share_in.shape[0]
    edge_width = w_left.shape[1]
    scale = (att_width // heads) ** (-0.5)
    live = table[slot, LIVE] > 0
    tiles = block // 8
    both_heads = 2 * heads

    @pl.when(slot == 0)
    def _():
        diag_s[...] = jnp.zeros_like(diag_s)

    @pl.when(jnp.logical_not(live))
    def _():
        recv_out[...] = jnp.zeros_like(recv_out)
        send_out[...] = jnp.zeros_like(send_out)

    @pl.when(live)
    def _():
        share, shift = share_in[...], shift_in[...]
        first_row = table[slot, RECV_BLOCK] * block
        first_frame = fill_bases(base_s, frames_here, first_row, frames_send, right_in[...], edge_gain)
        grad_right_s[...] = jnp.zeros_like(grad_right_s)
        even_s[...] = jnp.zeros_like(even_s)
        odd_s[...] = jnp.zeros_like(odd_s)
        rows_s[: GROUP * both_heads, :] = jnp.zeros((GROUP * both_heads, block), F32)
        lane = lax.broadcasted_iota(jnp.int32, (heads, block), 1)
        groups = block // GROUP

        def row_stage(at):
            for k in range(GROUP):
                i = at * GROUP + k
                here = lane == i
                factor = jnp.sum(jnp.where(here, share, 0.0), axis=1, keepdims=True)
                moved = jnp.sum(jnp.where(here, shift, 0.0), axis=1, keepdims=True)
                row = pl.multiple_of(i * both_heads, both_heads)
                probs = probs_in[pl.ds(row, heads), :]
                centred = probs_in[pl.ds(row + heads, heads), :]
                rows_s[pl.ds(row, heads), :] = (centred + moved * probs) * factor
                rows_s[pl.ds(row + heads, heads), :] = probs * factor

        def edge_stage(at, d_edge_s):
            first = pl.multiple_of(at * GROUP * both_heads, GROUP * both_heads)
            across = rows_s[pl.ds(first, GROUP * both_heads), :].T.astype(BF16)
            for k in range(GROUP):
                row = pl.multiple_of((at * GROUP + k) * both_heads, both_heads)
                diag_s[both_heads * k : both_heads * (k + 1), edge_width * k : edge_width * (k + 1)] = (
                    pair_in[pl.ds(row, both_heads), :]
                )
            for col in range(0, GROUP * edge_width, 2 * edge_width):
                d_edge_s[:, col : col + 2 * edge_width] = dot(across, diag_s[:, col : col + 2 * edge_width])

        def slope_stage(at, d_edge_s):
            base_of = [
                pl.multiple_of((frames_here[first_row + at * GROUP + k] - first_frame) * block, block)
                for k in range(GROUP)
            ]
            left_of = [
                jnp.broadcast_to(left_in[pl.ds(at * GROUP + k, 1), :], (8, edge_width)) for k in range(GROUP)
            ]
            left_sums = [jnp.zeros((8, edge_width), F32) for _ in range(GROUP)]
            for tile in range(tiles):
                span = slice(8 * tile, 8 * tile + 8)
                right_sum = grad_right_s[span, :]
                for k in range(GROUP):
                    half = base_s[pl.ds(base_of[k] + 8 * tile, 8), :] + left_of[k]
                    tanh = jnp.tanh(half)
                    slope = (1.0 + tanh) * (half - half * tanh + 1.0)
                    d_pre = slope * d_edge_s[span, edge_width * k : edge_width * (k + 1)]
                    right_sum = right_sum + d_pre
                    left_sums[k] = left_sums[k] + d_pre
                grad_right_s[span, :] = right_sum
            for k in range(GROUP):
                grad_left_s[pl.ds(at * GROUP + k, 1), :] = jnp.sum(left_sums[k], axis=0, keepdims=True)

        buffers = (even_s, odd_s)

        def step(two, carry):
            for parity in range(2):
                at = 2 * two + parity
                slope_stage(jnp.clip(at - 2, 0, groups - 1), buffers[parity])
                edge_stage(jnp.clip(at - 1, 0, groups - 1), buffers[1 - parity])
                row_stage(jnp.clip(at, 0, groups - 1))
            return carry

        lax.fori_loop(0, (groups + 2) // 2, step, 0)
        query, keys, d_att = query_in[...], keys_in[...], datt_in[...]
        head_of_lane = head_lanes(heads, att_width, block)
        grad_query = jnp.zeros((block, att_width), F32)
        grad_keys = jnp.zeros((block, att_width), F32)
        grad_values = jnp.zeros((block, att_width), F32)
        for h in range(heads):
            this = head_of_lane == h
            d_logit = rows_s[pl.ds(h, block, stride=both_heads), :].astype(BF16)
            weight = rows_s[pl.ds(heads + h, block, stride=both_heads), :].astype(BF16)
            grad_query = jnp.where(this, dot(d_logit, keys), grad_query)
            grad_keys = jnp.where(this, dot(d_logit.T, query), grad_keys)
            grad_values = jnp.where(this, dot(weight.T, d_att), grad_values)
        recv_out[...] = dot_t((grad_query * scale).astype(BF16), w_query[...]) + dot_t(
            (grad_left_s[...] * 0.5).astype(BF16), w_left[...]
        )
        send_out[...] = (
            dot_t((grad_keys * scale).astype(BF16), w_key[...])
            + dot_t(grad_values.astype(BF16), w_value[...])
            + dot_t((grad_right_s[...] * 0.5).astype(BF16), w_right[...])
        ).astype(BF16)


def pack_kernel(slot_of_owner, send_part, early, nodes_piece, w_out, message, mixed_piece):
    n_recv, _, att_width = message.shape
    block = send_part.shape[1]
    rows = nodes_piece.shape[0]
    total = early[0].astype(F32)
    for s in range(1, early.shape[0]):
        total += early[s].astype(F32)
    attended = total[:rows].astype(BF16)
    mixed_piece[...] = (nodes_piece[...].astype(F32) + dot(attended, w_out[...])).astype(BF16)
    extra = total[rows:].astype(BF16)

    for r in range(n_recv):
        slot = slot_of_owner[r]

        @pl.when(slot >= 0)
        def _():
            message[r, :block, :] = send_part[jnp.maximum(slot, 0)]

        @pl.when(slot < 0)
        def _():
            message[r, :block, :] = jnp.zeros((block, att_width), BF16)

        message[r, block:, :] = extra


def merge_kernel(
    table, requested, back, recv_part, send_part, mixed_piece, message, bias_out, acc_s
):
    n_recv, _, att_width = back.shape
    slots, block, _ = recv_part.shape
    n_send = message.shape[0]
    rows = mixed_piece.shape[0]
    acc_s[...] = jnp.zeros_like(acc_s)
    for p in range(slots):
        at = pl.multiple_of(table[p, RECV_BLOCK] * block, block)
        acc_s[pl.ds(at, block), :] += recv_part[p]

        @pl.when(table[p, IS_LOCAL] > 0)
        def _():
            to = pl.multiple_of(table[p, LOCAL_BLOCK] * block, block)
            acc_s[pl.ds(to, block), :] += send_part[p].astype(F32)

    extra = jnp.zeros((back.shape[1] - block, att_width), F32)
    for r in range(n_recv):
        extra += back[r, block:, :].astype(F32)

        @pl.when(requested[r] > 0)
        def _():
            to = pl.multiple_of((requested[r] - 1) * block, block)
            acc_s[pl.ds(to, block), :] += back[r, :block, :].astype(F32)

    edge_rows = message.shape[1] - 2 * rows
    for s in range(n_send):
        message[s, :rows, :] = acc_s[s * rows : (s + 1) * rows, :].astype(BF16)
        message[s, rows : 2 * rows, :] = mixed_piece[...]
        message[s, 2 * rows :, :] = extra[:edge_rows].astype(BF16)
    bias_out[...] = extra[edge_rows:, : bias_out.shape[1]]


def last_kernel(parts, d_out_piece, grad_piece):
    rows = d_out_piece.shape[0]
    total = d_out_piece[...].astype(F32)
    for s in range(parts.shape[0]):
        total += parts[s, :rows, :].astype(F32)
    out = total.astype(grad_piece.dtype)
    for s in range(grad_piece.shape[0]):
        grad_piece[s] = out


def params():
    return pltpu.CompilerParams(vmem_limit_bytes=VMEM_LIMIT)


def whole(*shape):
    return pl.BlockSpec(shape, lambda *_: (0,) * len(shape))


def body(
    nodes,
    frames,
    pairs,
    masks,
    d_out,
    w_query,
    w_key,
    w_value,
    w_left,
    w_right,
    frame_edge,
    w_bias,
    w_edge_value,
    w_out,
):
    rows, width = nodes.shape
    slots, block = masks.shape
    nb_local = rows // block
    heads, edge_width = w_bias.shape
    att_width = w_query.shape[1]
    my_recv = lax.axis_index("recv")
    my_send = lax.axis_index("send")
    n_recv = lax.axis_size("recv")
    n_send = lax.axis_size("send")
    base_block = my_recv * nb_local
    piece = rows // n_send
    edge_piece = edge_width // n_send

    recv_blocks, send_blocks = pairs[0], pairs[1]
    owners = send_blocks // nb_local
    is_local = owners == my_recv
    live = jnp.any(masks > 0, axis=1)
    hits = (owners[None, :] == jnp.arange(n_recv, dtype=jnp.int32)[:, None]) & ~is_local[None, :]
    wanted = jnp.sum(jnp.where(hits, (send_blocks % nb_local)[None, :] + 1, 0), axis=1)
    slot_of_owner = jnp.sum(jnp.where(hits, jnp.arange(slots, dtype=jnp.int32)[None, :] + 1, 0), axis=1) - 1
    requested = lax.all_to_all(wanted, "recv", split_axis=0, concat_axis=0, tiled=True)
    table = jnp.stack(
        [
            recv_blocks - base_block,
            jnp.where(is_local, send_blocks - base_block, 0),
            jnp.where(is_local, 0, owners),
            is_local.astype(jnp.int32),
            send_blocks,
            live.astype(jnp.int32),
        ],
        axis=1,
    )
    node_blocks = nodes.reshape(nb_local, block, width)
    replies = jnp.take(node_blocks, jnp.maximum(requested - 1, 0), axis=0)
    got = lax.all_to_all(replies, "recv", split_axis=0, concat_axis=0, tiled=True)

    frames_here = lax.dynamic_slice_in_dim(frames, my_recv * rows, rows)
    frame_rows = frames.reshape(frames.shape[0] // block, 1, block)
    gain = frame_edge.reshape(1, edge_width)
    d_out_blocks = d_out.reshape(nb_local, block, width)

    def per_slot(*shape):
        return pl.BlockSpec((None, *shape), lambda p, *_: (p,) + (0,) * len(shape))

    def shape_of(dtype, *shape):
        return jax.ShapeDtypeStruct((slots, *shape), dtype)

    both = 2 * heads
    outs = (
        (F32, block * both, block),
        (BF16, block * both, edge_width),
        (F32, block * both, edge_width),
        (F32, 4, heads, block),
        (F32, block, att_width),
        (BF16, block, att_width),
        (BF16, block, att_width),
        (BF16, block, att_width),
        (F32, block, edge_width),
        (F32, block, edge_width),
    )
    own_spec = pl.BlockSpec((None, block, width), lambda p, t, f: (t[p, RECV_BLOCK], 0, 0))
    frame_spec = pl.BlockSpec((None, 1, block), lambda p, t, f: (t[p, SEND_BLOCK], 0, 0))
    probs, pair_rows, ctx, stats, att, query, keys, d_att, left, right = pl.pallas_call(
        first_kernel,
        out_shape=tuple(shape_of(*o) for o in outs),
        grid_spec=pltpu.PrefetchScalarGridSpec(
            num_scalar_prefetch=2,
            grid=(slots,),
            in_specs=[
                own_spec,
                pl.BlockSpec((None, block, width), lambda p, t, f: (t[p, LOCAL_BLOCK], 0, 0)),
                pl.BlockSpec((None, block, width), lambda p, t, f: (t[p, OWNER], 0, 0)),
                own_spec,
                frame_spec,
                per_slot(1, block),
                whole(width, att_width),
                whole(width, att_width),
                whole(width, att_width),
                whole(width, edge_width),
                whole(width, edge_width),
                whole(edge_width, att_width),
                whole(att_width, width),
                whole(1, edge_width),
                whole(heads, edge_width),
            ],
            out_specs=[per_slot(*o[1:]) for o in outs],
            scratch_shapes=[
                pltpu.VMEM((block * heads, block), F32),
                pltpu.VMEM((block * heads, block), F32),
                pltpu.VMEM((block * heads, edge_width), F32),
                pltpu.VMEM((block, att_width), F32),
                pltpu.VMEM((block, att_width), F32),
                pltpu.VMEM((2 * block, att_width), BF16),
                pltpu.VMEM((block * block, edge_width), BF16),
                pltpu.VMEM((block * both, block), F32),
                pltpu.VMEM((block * block, edge_width), F32),
            ],
        ),
        compiler_params=params(),
        name="first",
    )(
        table, frames_here, node_blocks, node_blocks, got, d_out_blocks, frame_rows,
        masks.reshape(slots, 1, block), w_query, w_key, w_value, w_left, w_right,
        w_edge_value, w_out, gain, w_bias,
    )

    stats_all = lax.all_gather(stats, "send", axis=0, tiled=True)
    early_rows = piece + edge_piece + heads
    share, shift, early_out = pl.pallas_call(
        mid_kernel,
        out_shape=(
            shape_of(F32, heads, block),
            shape_of(F32, heads, block),
            jax.ShapeDtypeStruct((n_send, early_rows, att_width), BF16),
        ),
        grid_spec=pltpu.PrefetchScalarGridSpec(
            num_scalar_prefetch=1,
            grid=(slots,),
            in_specs=[
                whole(slots * n_send, 4, heads, block),
                per_slot(4, heads, block),
                per_slot(block * both, edge_width),
                per_slot(block, att_width),
                per_slot(block, att_width),
            ],
            out_specs=[
                per_slot(heads, block),
                per_slot(heads, block),
                whole(n_send, early_rows, att_width),
            ],
            scratch_shapes=[
                pltpu.VMEM((rows, att_width), F32),
                pltpu.VMEM((att_width, edge_width), F32),
                pltpu.VMEM((heads, edge_width), F32),
            ],
        ),
        compiler_params=params(),
        name="mid",
    )(table, stats_all, stats, ctx, att, d_att)
    early = lax.all_to_all(early_out, "send", split_axis=0, concat_axis=0, tiled=True)

    recv_part, send_part = pl.pallas_call(
        grad_kernel,
        out_shape=(shape_of(F32, block, att_width), shape_of(BF16, block, att_width)),
        grid_spec=pltpu.PrefetchScalarGridSpec(
            num_scalar_prefetch=2,
            grid=(slots,),
            in_specs=[
                per_slot(heads, block),
                per_slot(heads, block),
                per_slot(block * both, block),
                per_slot(block * both, edge_width),
                per_slot(block, att_width),
                per_slot(block, att_width),
                per_slot(block, att_width),
                per_slot(block, edge_width),
                per_slot(block, edge_width),
                frame_spec,
                whole(width, att_width),
                whole(width, att_width),
                whole(width, att_width),
                whole(width, edge_width),
                whole(width, edge_width),
                whole(1, edge_width),
            ],
            out_specs=[per_slot(block, att_width), per_slot(block, att_width)],
            scratch_shapes=[
                pltpu.VMEM((block * both, block), F32),
                pltpu.VMEM((GROUP * both, GROUP * edge_width), BF16),
                pltpu.VMEM((block, GROUP * edge_width), F32),
                pltpu.VMEM((block, GROUP * edge_width), F32),
                pltpu.VMEM((block * block, edge_width), F32),
                pltpu.VMEM((block, edge_width), F32),
                pltpu.VMEM((block, edge_width), F32),
            ],
        ),
        compiler_params=params(),
        cost_estimate=pl.CostEstimate(flops=40_000_000_000, bytes_accessed=12_000_000, transcendentals=8_000_000),
        name="grad",
    )(
        table, frames_here, share, shift, probs, pair_rows, query, keys, d_att, left, right, frame_rows,
        w_query, w_key, w_value, w_left, w_right, gain,
    )

    nodes_piece = lax.dynamic_slice_in_dim(nodes, my_send * piece, piece)
    d_out_piece = lax.dynamic_slice_in_dim(d_out, my_send * piece, piece)
    smem = pl.BlockSpec(memory_space=pltpu.SMEM)
    vmem = pl.BlockSpec(memory_space=pltpu.VMEM)
    message, mixed_piece = pl.pallas_call(
        pack_kernel,
        out_shape=(
            jax.ShapeDtypeStruct((n_recv, block + edge_piece + heads, att_width), BF16),
            jax.ShapeDtypeStruct((piece, width), BF16),
        ),
        in_specs=[smem, vmem, vmem, vmem, vmem],
        out_specs=(vmem, vmem),
        compiler_params=params(),
        name="pack",
    )(slot_of_owner, send_part, early, nodes_piece, w_out)
    back = lax.all_to_all(message, "recv", split_axis=0, concat_axis=0, tiled=True)
    message, grad_bias = pl.pallas_call(
        merge_kernel,
        out_shape=(
            jax.ShapeDtypeStruct((n_send, 2 * piece + edge_piece, att_width), BF16),
            jax.ShapeDtypeStruct((heads, edge_width), F32),
        ),
        in_specs=[smem, smem, vmem, vmem, vmem, vmem],
        out_specs=(vmem, vmem),
        scratch_shapes=[pltpu.VMEM((rows, att_width), F32)],
        compiler_params=params(),
        name="merge",
    )(table, requested, back, recv_part, send_part, mixed_piece)
    parts = lax.all_to_all(message, "send", split_axis=0, concat_axis=0, tiled=True)
    grad_out = pl.pallas_call(
        last_kernel,
        out_shape=jax.ShapeDtypeStruct((n_send, piece, width), BF16),
        in_specs=[vmem, vmem],
        out_specs=vmem,
        compiler_params=params(),
        name="last",
    )(parts, d_out_piece)
    grad_nodes = lax.all_to_all(grad_out, "send", split_axis=0, concat_axis=0, tiled=True)
    mixed = parts[:, piece : 2 * piece].reshape(rows, width)
    grad_edge_value = parts[:, 2 * piece :].reshape(edge_width, att_width).astype(F32)
    return (mixed, grad_nodes.reshape(rows, width).astype(F32), grad_bias, grad_edge_value)


def solution(mesh):
    in_specs = (
        P("recv", None),
        P(),
        P(None, ("recv", "send")),
        P(("recv", "send"), None),
        P("recv", None),
        P(),
        P(),
        P(),
        P(),
        P(),
        P(),
        P(),
        P(),
        P(),
    )
    out_specs = (P("recv", None), P("recv", None), P(), P())
    return jax.shard_map(body, mesh=mesh, in_specs=in_specs, out_specs=out_specs, check_vma=False)
```
